32 devices in a mesh: dp: 4 (over x, core), seq: 8 (over z, y).
Axes of the slice: x: 2, y: 2, z: 4, core: 2. Of those that a mesh axis runs over, the one named last changes fastest.
Arguments:
- inputs: bfloat16 [4, 1024, 1536], P('dp', 'seq'), may hold values from -6 to 6
- doc_lengths: int32 [4, 4], P('dp'), may hold values from 1 to 512, 1024 in all within a row
- w_query: bfloat16 [1536, 1536], P(('dp', 'seq')), may hold values from -0.15625 to 0.15625
- w_key: bfloat16 [1536, 1536], P(('dp', 'seq')), may hold values from -0.15625 to 0.15625
- w_value: bfloat16 [1536, 1536], P(('dp', 'seq')), may hold values from -0.15625 to 0.15625
- w_house: bfloat16 [1536, 1536], P(('dp', 'seq')), may hold values from -0.15625 to 0.15625
- w_beta: bfloat16 [1536, 12], P(('dp', 'seq')), may hold values from -0.15625 to 0.15625
- beta_bias: float32 [12], replicated, may hold values from -2 to 2
- norm_attn: bfloat16 [1536], P(('dp', 'seq')), may hold values from 0.5 to 1.5
- w_out: bfloat16 [1536, 1536], P(('dp', 'seq')), may hold values from -0.625 to 0.625
- norm_mlp: bfloat16 [1536], P(('dp', 'seq')), may hold values from 0.5 to 1.5
- w_gate: bfloat16 [1536, 4096], P(('dp', 'seq')), may hold values from -0.15625 to 0.15625
- w_up: bfloat16 [1536, 4096], P(('dp', 'seq')), may hold values from -0.15625 to 0.15625
- w_down: bfloat16 [4096, 1536], P(('dp', 'seq')), may hold values from -0.09375 to 0.09375
- grad_y: bfloat16 [4, 1024, 1536], P('dp', 'seq'), may hold values from -6 to 6
Outputs:
- outputs: bfloat16 [4, 1024, 1536], P('dp', 'seq')
- grad_x: float32 [4, 1024, 1536], P('dp', 'seq')
- grad_w_query: float32 [1536, 1536], P(('dp', 'seq'))
- grad_w_key: float32 [1536, 1536], P(('dp', 'seq'))
- grad_w_value: float32 [1536, 1536], P(('dp', 'seq'))
- grad_w_house: float32 [1536, 1536], P(('dp', 'seq'))
- grad_w_beta: float32 [1536, 12], P(('dp', 'seq'))
- grad_beta_bias: float32 [12], replicated
- grad_norm_attn: float32 [1536], P(('dp', 'seq'))
- grad_w_out: float32 [1536, 1536], P(('dp', 'seq'))
- grad_norm_mlp: float32 [1536], P(('dp', 'seq'))
- grad_w_gate: float32 [1536, 4096], P(('dp', 'seq'))
- grad_w_up: float32 [1536, 4096], P(('dp', 'seq'))
- grad_w_down: float32 [4096, 1536], P(('dp', 'seq'))
The draws below stay inside these ranges and needn't reach their ends.
Inputs may be any that keep to these rules, and one draw needn't show every extreme that they name: `doc_lengths`: in every row the 4 lengths add up to 1024, and the longest is exactly half of 1024.
All inputs are finite; a program needn't handle non-finite values.
Results may differ from the reference program's by a relative error of at most 0.02.
The reference program's roundings to bfloat16 on the way count: a program that leaves them out, or rounds other values in their place, can miss the bound.
Values may be sent and summed in bfloat16 or wider, within the bound.
No kernel may reach another device: no remote copies, remote signals or barrier semaphores. Data moves between devices by JAX's collectives and lax.ppermute only.
A program may use at most 320 MiB of HBM per device.

```python
import math
import jax
import jax.numpy as jnp
import numpy as np
from jax import lax

D = 1536
HEADS = 12
HEAD_DIM = 128
FF = 4096
BLOCK = 64
DOCS = 4
ROWS = 4
LEN = 1024


def levels(stream_key, dims, pieces, smallest, largest):
    def one(axis_at, shards_of):
        draws = jax.random.uniform(jax.random.fold_in(jax.random.fold_in(stream_key, 6), axis_at), (shards_of,), jnp.float32, smallest / len(pieces), largest / len(pieces))
        return jnp.repeat(jnp.exp(draws), dims[axis_at] // shards_of).reshape((-1,) + (1,) * (len(dims) - axis_at - 1))

    factor_of = one(*pieces[0])
    for cut in pieces[1:]:
        factor_of = factor_of * one(*cut)
    return factor_of


def length_profile(amount, total, limit, skew):
    portions = [(1 << 20) // math.isqrt(standing ** skew) + 1 for standing in range(2, amount + 1)]
    surplus, given = total - limit - (amount - 1), [1] * (amount - 1)
    while surplus > 0:
        free = [i for i in range(amount - 1) if given[i] < limit]
        mass, budget = sum([portions[i] for i in free]), surplus
        for i in free:
            extra = min(limit - given[i], max(1, budget * portions[i] // mass), surplus)
            given[i] = given[i] + extra
            surplus = surplus - extra
    return np.array([limit] + given)


def uneven_parts(key, count, total, most, slope):
    if count == 2:
        one = jax.random.randint(key, (), max(1, total - most), min(most, total - 1) + 1)
        return jnp.stack([one, total - one])
    lengths = jnp.asarray(length_profile(count, total, most, slope), jnp.int32)
    twos = (count - 1) // 2
    donor, taker = lengths[1:1 + 2 * twos:2], lengths[2:2 + 2 * twos:2]
    margin = jnp.minimum(donor - 1, most - taker)
    shifted = jax.random.randint(jax.random.fold_in(key, 1), (twos,), 0, 1 << 20) % (margin + 1)
    lengths = lengths.at[1:1 + 2 * twos:2].set(donor - shifted).at[2:2 + 2 * twos:2].set(taker + shifted)
    return lengths[jax.random.permutation(jax.random.fold_in(key, 2), count)]


def bell_draw(rng, extent, width, reach, cuts=(), held_as=jnp.bfloat16):
    gain = levels(rng, extent, cuts, -0.22, 0.18) if cuts else 1.0
    entries = jax.random.normal(rng, extent, jnp.float32) * width * gain
    return jnp.minimum(jnp.maximum(entries, -reach), reach).astype(held_as)


def setup_inputs(seed: int = 0) -> dict:
    splits = jax.random.split(jax.random.key(seed), 16)
    inputs = bell_draw(splits[0], (ROWS, LEN, D), 1.0, 6.0, ((0, 4), (1, 8)))
    doc_lengths = jax.vmap(lambda own: uneven_parts(own, DOCS, LEN, LEN // 2, 2))(jax.random.split(splits[1], ROWS)).reshape((ROWS, DOCS)).astype(jnp.int32)
    w_query = bell_draw(splits[2], (D, D), D ** -0.5, 0.15625, ((0, 32),))
    w_key = bell_draw(splits[3], (D, D), D ** -0.5, 0.15625, ((0, 32),))
    w_value = bell_draw(splits[4], (D, D), D ** -0.5, 0.15625, ((0, 32),))
    w_house = bell_draw(splits[5], (D, D), D ** -0.5, 0.15625, ((0, 32),))
    w_beta = bell_draw(splits[6], (D, HEADS), D ** -0.5, 0.15625, ((0, 32),))
    beta_bias = jnp.clip(jax.random.uniform(splits[7], (HEADS,), jnp.float32, -2.0, 2.0), -2.0, 2.0)
    norm_attn = jnp.clip(1.0 + 0.1 * jax.random.normal(splits[8], (D,), jnp.float32), 0.5, 1.5).astype(jnp.bfloat16)
    w_out = bell_draw(splits[9], (D, D), (D // 16) ** -0.5, 0.625, ((0, 32),))
    norm_mlp = jnp.clip(1.0 + 0.1 * jax.random.normal(splits[10], (D,), jnp.float32), 0.5, 1.5).astype(jnp.bfloat16)
    w_gate = bell_draw(splits[11], (D, FF), D ** -0.5, 0.15625, ((0, 32),))
    w_up = bell_draw(splits[12], (D, FF), D ** -0.5, 0.15625, ((0, 32),))
    w_down = bell_draw(splits[13], (FF, D), FF ** -0.5, 0.09375, ((0, 32),))
    grad_y = bell_draw(splits[14], (ROWS, LEN, D), 1.0, 6.0, ((0, 4), (1, 8)))
    return {"inputs": inputs, "doc_lengths": doc_lengths, "w_query": w_query, "w_key": w_key, "w_value": w_value, "w_house": w_house, "w_beta": w_beta, "beta_bias": beta_bias, "norm_attn": norm_attn, "w_out": w_out, "norm_mlp": norm_mlp, "w_gate": w_gate, "w_up": w_up, "w_down": w_down, "grad_y": grad_y}


EPS = 1e-06
HIGH = lax.Precision.HIGHEST

@jax.custom_vjp
def low(v):
    return lax.optimization_barrier(v.astype(jnp.bfloat16)).astype(jnp.float32)

@jax.custom_vjp
def low_back(v):
    return v

def low_keep(v):
    return (low(v), None)

def low_pass(kept, grad):
    return (grad,)

def back_keep(v):
    return (v, None)

def back_low(kept, grad):
    return (low(grad),)
low.defvjp(low_keep, low_pass)
low_back.defvjp(back_keep, back_low)

def rms_norm(values, gains):
    return values * lax.rsqrt(lax.optimization_barrier(jnp.mean(values * values, axis=-1, keepdims=True)) + EPS) * gains

def block_factors(queries, keys_in, houses, beta_rate):
    block_len = queries.shape[-2]
    rows_at = jnp.arange(block_len)[:, None]
    cols_at = jnp.arange(block_len)[None, :]
    house_gram = jnp.einsum('...ie,...je->...ij', houses, houses, precision=HIGH)
    lower_tri = jnp.eye(block_len, dtype=jnp.float32) + jnp.where(rows_at > cols_at, beta_rate[..., :, None] * house_gram, 0.0)
    unit_matrix = jnp.broadcast_to(jnp.eye(block_len, dtype=jnp.float32), lower_tri.shape)
    inverse = jax.scipy.linalg.solve_triangular(lower_tri, unit_matrix, lower=True, unit_diagonal=True)
    factor = inverse * beta_rate[..., None, :]
    query_house = jnp.where(rows_at >= cols_at, jnp.einsum('...ie,...se->...is', queries, houses, precision=HIGH), 0.0)
    house_key = jnp.where(rows_at > cols_at, jnp.einsum('...re,...je->...rj', houses, keys_in, precision=HIGH), 0.0)
    left_factor = jnp.einsum('...is,...sr->...ir', query_house, factor, precision=HIGH)
    factor_right = jnp.einsum('...sr,...rj->...sj', factor, house_key, precision=HIGH)
    local_raw = jnp.einsum('...ie,...je->...ij', queries, keys_in, precision=HIGH) - jnp.einsum('...ir,...rj->...ij', left_factor, house_key, precision=HIGH)
    query_moved = low(queries - jnp.einsum('...ir,...re->...ie', left_factor, houses, precision=HIGH))
    key_moved = low(keys_in - jnp.einsum('...sj,...se->...je', factor_right, houses, precision=HIGH))
    mixing = jnp.einsum('...sr,...se->...re', factor, houses, precision=HIGH)
    return (query_moved, key_moved, mixing, local_raw)

def carry_through(keys_now, houses, mixing):
    project = jnp.einsum('...me,...re->...mr', keys_now, houses, precision=HIGH)
    return low(keys_now - jnp.einsum('...mr,...re->...me', project, mixing, precision=HIGH))

def attend(queries, keys_in, values, houses, beta_rates, doc_ids):
    length = queries.shape[0]
    blocks = length // BLOCK

    def to_blocks(source_arr):
        return jnp.swapaxes(source_arr.reshape((blocks, BLOCK) + source_arr.shape[1:]), 1, 2)
    q_blocks = to_blocks(queries)
    k_blocks = to_blocks(keys_in)
    v_blocks = to_blocks(values)
    h_blocks = to_blocks(houses)
    r_blocks = to_blocks(beta_rates)
    moved_q, moved_k, mixing, local_raw = jax.vmap(block_factors)(q_blocks, k_blocks, h_blocks, r_blocks)
    key_pos = jnp.arange(length).reshape(blocks, BLOCK)
    key_doc = doc_ids.reshape(blocks, BLOCK)
    scale_by = HEAD_DIM ** (-0.5)
    slot_ids = jnp.arange(blocks)

    def one_block(key_stack, item_in):
        block_at, query_b, key_b, house_b, mixing_b, local_b = item_in
        cross_raw = jnp.einsum('hie,nhje->hinj', query_b, key_stack, precision=HIGH)
        raw_all = jnp.where((slot_ids == block_at)[None, None, :, None], local_b[:, :, None, :], cross_raw)
        scores = low_back(raw_all * scale_by)
        query_pos = block_at * BLOCK + jnp.arange(BLOCK)
        query_doc = lax.dynamic_slice_in_dim(doc_ids, block_at * BLOCK, BLOCK)
        valid_at = (key_pos[None] <= query_pos[:, None, None]) & (key_doc[None] == query_doc[:, None, None])
        masked = jnp.where(valid_at[None], scores, -1e+30)
        row_peak = lax.optimization_barrier(jnp.max(masked, axis=(2, 3), keepdims=True))
        weight = jnp.exp(masked - row_peak)
        soft_prob = weight / lax.optimization_barrier(jnp.sum(weight, axis=(2, 3), keepdims=True))
        out_b = jnp.einsum('hinj,nhje->hie', low(soft_prob), v_blocks, precision=HIGH)
        key_stack = carry_through(key_stack, house_b, mixing_b)
        key_stack = jnp.where((slot_ids == block_at)[:, None, None, None], key_b[None], key_stack)
        return (key_stack, out_b)
    stack_zero = jnp.zeros((blocks,) + k_blocks.shape[1:], jnp.float32)
    block_items = (jnp.arange(blocks, dtype=jnp.int32), moved_q, moved_k, h_blocks, mixing, local_raw)
    unused, outputs_b = lax.scan(jax.checkpoint(one_block), stack_zero, block_items)
    return jnp.swapaxes(outputs_b, 1, 2).reshape(length, HEADS * HEAD_DIM)

def forward(x_in, w_query, w_key, w_value, w_house, w_beta, beta_bias, norm_attn, w_out, norm_mlp, w_gate, w_up, w_down, doc_ids):
    normed = low(rms_norm(x_in, norm_attn))
    queries = low(low_back(jnp.dot(normed, w_query, precision=HIGH)))
    keys_all = low(low_back(jnp.dot(normed, w_key, precision=HIGH)))
    values = low(low_back(jnp.dot(normed, w_value, precision=HIGH)))
    house_raw = low_back(jnp.dot(normed, w_house, precision=HIGH))
    logits = low_back(jnp.dot(normed, w_beta, precision=HIGH)) + beta_bias
    beta_rates = 2.0 * jax.nn.sigmoid(logits)
    head_shape = x_in.shape[:2] + (HEADS, HEAD_DIM)
    house_heads = house_raw.reshape(head_shape)
    houses = low(house_heads * lax.rsqrt(lax.optimization_barrier(jnp.sum(house_heads * house_heads, axis=-1, keepdims=True)) + EPS))
    mixed_out = lax.map(lambda item_in: attend(item_in[0], item_in[1], item_in[2], item_in[3], item_in[4], item_in[5]), (queries.reshape(head_shape), keys_all.reshape(head_shape), values.reshape(head_shape), houses, beta_rates, doc_ids))
    attn_out = low(low_back(mixed_out))
    branch = low_back(jnp.dot(attn_out, w_out, precision=HIGH))
    middle = x_in + branch
    normed_mlp = low(rms_norm(middle, norm_mlp))
    gate_val = low_back(jnp.dot(normed_mlp, w_gate, precision=HIGH))
    up_val = low_back(jnp.dot(normed_mlp, w_up, precision=HIGH))
    hidden = low(jax.nn.silu(gate_val) * up_val)
    return middle + jnp.dot(hidden, w_down, precision=HIGH)

def reference(inputs, doc_lengths, w_query, w_key, w_value, w_house, w_beta, beta_bias, norm_attn, w_out, norm_mlp, w_gate, w_up, w_down, grad_y):
    length = inputs.shape[1]
    doc_ends = jnp.cumsum(doc_lengths, axis=-1)
    doc_ids = lax.optimization_barrier(jnp.sum((jnp.arange(length)[None, :, None] >= doc_ends[:, None, :]).astype(jnp.int32), axis=-1))
    params = tuple((item.astype(jnp.float32) for item in (inputs, w_query, w_key, w_value, w_house, w_beta, beta_bias, norm_attn, w_out, norm_mlp, w_gate, w_up, w_down)))
    result, pull_back = jax.vjp(lambda *args_in: forward(*args_in, doc_ids), *params)
    gradients = pull_back(grad_y.astype(jnp.float32))
    return (result.astype(jnp.bfloat16), gradients[0], gradients[1], gradients[2], gradients[3], gradients[4], gradients[5], gradients[6], gradients[7], gradients[8], gradients[9], gradients[10], gradients[11], gradients[12])
```

```python
import functools
import jax, jax.numpy as jnp
from jax import lax
from jax.experimental import pallas as pl
from jax.experimental.pallas import tpu as pltpu

bf16=jnp.bfloat16; f32=jnp.float32
E_=128; BLOCK=64; PAIR=128; CHUNK=256
EPS=1e-6
SCALE=128**-0.5

def mm(a,b,ca,cb):
    return lax.dot_general(a,b,(((ca,),(cb,)),((),())),preferred_element_type=f32)
def halves(a):
    hi=a.astype(bf16)
    return hi,(a-hi.astype(f32)).astype(bf16)
def mm_x(a,b,ca,cb):
    h,l=halves(a)
    return mm(h,b,ca,cb)+mm(l,b,ca,cb)
def mm_y(a,b,ca,cb):
    h,l=halves(b)
    return mm(a,h,ca,cb)+mm(a,l,ca,cb)
def mm_xy(a,b,ca,cb):
    ah,al=halves(a); bh,bl=halves(b)
    return mm(ah,bh,ca,cb)+(mm(ah,bl,ca,cb)+mm(al,bh,ca,cb))

def pair_masks():
    r=lax.broadcasted_iota(jnp.int32,(PAIR,PAIR),0)
    c=lax.broadcasted_iota(jnp.int32,(PAIR,PAIR),1)
    same=(r//BLOCK)==(c//BLOCK)
    return r,c,same

def col_to_row(col,eye):
    return jnp.sum(jnp.where(eye,col,0.0),axis=0,keepdims=True)

def inverse_of(a,r,c):
    eye=(r==c).astype(f32)
    x=eye-jnp.where((r//2)==(c//2),a,0.0)
    size=2
    while size<BLOCK:
        part=jnp.where(((r//(2*size))==(c//(2*size)))&((r//size)!=(c//size)),a,0.0)
        x=x-mm_xy(mm_xy(x,part,1,0),x,1,0)
        size*=2
    return x

def factors_of(q,k,w,beta,x,r,c,same):
    eye=r==c
    t=x*col_to_row(beta,eye)
    xq=jnp.where(same&(r>=c),mm(q,w,1,1),0.0)
    y=jnp.where(same&(r>c),mm(w,k,1,1),0.0)
    xt=mm_xy(xq,t,1,0)
    ty=mm_xy(t,y,1,0)
    return t,xq,y,xt,ty

def head_inputs(proj_ref,rows,h,nh):
    q=proj_ref[rows,h*E_:(h+1)*E_].astype(bf16)
    k=proj_ref[rows,(nh+h)*E_:(nh+h+1)*E_].astype(bf16)
    hr=proj_ref[rows,(3*nh+h)*E_:(3*nh+h+1)*E_]
    ex=proj_ref[rows,4*nh*E_:(4*nh+1)*E_]
    lane=lax.broadcasted_iota(jnp.int32,ex.shape,1)
    logit=jnp.sum(jnp.where(lane==h,ex,0.0),axis=1,keepdims=True)
    return q,k,hr,logit

def factor_kernel(nh,proj_ref,bias_ref,w_ref,qm_ref,kmp_ref,kmf_ref,mix_ref,loc_ref,x_ref):
    r,c,same=pair_masks()
    for h in range(nh):
        q,k,hr,logit=head_inputs(proj_ref,slice(None),h,nh)
        beta=2.0*jax.nn.sigmoid(logit+bias_ref[h])
        w=(hr*lax.rsqrt(jnp.sum(hr*hr,axis=1,keepdims=True)+EPS)).astype(bf16)
        a=jnp.where(same&(r>c),beta*mm(w,w,1,1),0.0)
        x=inverse_of(a,r,c)
        t,xq,y,xt,ty=factors_of(q,k,w,beta,x,r,c,same)
        qm=(q.astype(f32)-mm_x(xt,w,1,0)).astype(bf16)
        kmp=(k.astype(f32)-mm_x(ty,w,0,0)).astype(bf16)
        mix=mm_x(t,w,0,0)
        inner=mm(q,k,1,1)-mm_xy(xt,y,1,0)
        cross=mm(qm,kmp,1,1)
        loc=jnp.where(same,inner,cross)
        p=jnp.where((r<BLOCK)&(c>=BLOCK),mm(kmp,w,1,1),0.0)
        kmf=(kmp.astype(f32)-mm_xy(p,mix,1,0)).astype(bf16)
        w_ref[h]=w; qm_ref[h]=qm; kmp_ref[h]=kmp; kmf_ref[h]=kmf
        mix_ref[h]=mix; loc_ref[h]=loc; x_ref[h]=x

def run_factors(proj,bias,nh):
    L=proj.shape[0]; wd=proj.shape[1]
    blk=pl.BlockSpec((nh,PAIR,E_),lambda g:(0,g,0))
    o=lambda dt: jax.ShapeDtypeStruct((nh,L,E_),dt)
    return pl.pallas_call(functools.partial(factor_kernel,nh),
        grid=(L//PAIR,),
        in_specs=[pl.BlockSpec((PAIR,wd),lambda g:(g,0)),pl.BlockSpec(memory_space=pltpu.SMEM)],
        out_specs=[blk]*7,
        out_shape=[o(bf16),o(bf16),o(bf16),o(bf16),o(f32),o(f32),o(f32)],
        cost_estimate=pl.CostEstimate(flops=L//PAIR*nh*60*2*128**3,bytes_accessed=L*wd*4+nh*L*128*20,transcendentals=0),
    )(proj,bias)

def start_of(ends_ref,docs,pos):
    s=jnp.zeros_like(pos)
    for d in range(docs):
        s=jnp.maximum(s,jnp.where(pos>=ends_ref[d],ends_ref[d],0))
    return s

def scalar_start(ends_ref,docs,pos):
    s=jnp.int32(0)
    for d in range(docs):
        s=jnp.maximum(s,jnp.where(pos>=ends_ref[d],ends_ref[d],0))
    return s

def tile_pos(g,shape):
    return g*PAIR+lax.broadcasted_iota(jnp.int32,shape,0)

def chunk_range(ends_ref,docs,g):
    lo=scalar_start(ends_ref,docs,g*PAIR)//CHUNK
    hi=(g*PAIR+CHUNK-1)//CHUNK
    return lo,hi

def carried_forward(st,w,mh,ml):
    ph,pl_=halves(mm(st,w,1,1))
    return (st.astype(f32)-(mm(ph,mh,1,0)+(mm(ph,ml,1,0)+mm(pl_,mh,1,0)))).astype(bf16)

def forward_kernel(nh,docs,ends_ref,qm_ref,kmf_ref,w_ref,mix_ref,loc_ref,v_ref,
                   out_ref,lse_ref,hist_ref,stack,sbuf):
    g=pl.program_id(0)
    @pl.when(g==0)
    def _():
        stack[...]=jnp.zeros_like(stack)
    lo,hi=chunk_range(ends_ref,docs,g)
    rowstart=start_of(ends_ref,docs,tile_pos(g,(PAIR,PAIR)))
    cc=lax.broadcasted_iota(jnp.int32,(PAIR,PAIR),1)
    rr=lax.broadcasted_iota(jnp.int32,(PAIR,PAIR),0)
    okd=(cc<=rr)&(cc+g*PAIR>=rowstart)
    sd=[jnp.where(okd,loc_ref[h]*SCALE,-1e30) for h in range(nh)]
    peak=tuple(jnp.max(s,axis=1,keepdims=True) for s in sd)
    start2=start_of(ends_ref,docs,tile_pos(g,(PAIR,CHUNK)))
    c2=lax.broadcasted_iota(jnp.int32,(PAIR,CHUNK),1)
    mixs=[[halves(mix_ref[h,b*BLOCK:(b+1)*BLOCK]) for b in range(2)] for h in range(nh)]
    def step(c,pk):
        rows=pl.ds(pl.multiple_of(c*CHUNK,CHUNK),CHUNK)
        ok=(c2+c*CHUNK>=start2)&(c2+c*CHUNK<g*PAIR)
        new=[]
        for h in range(nh):
            st0=stack[h,rows,:]
            st1=carried_forward(st0,w_ref[h,0:BLOCK],*mixs[h][0])
            st2=carried_forward(st1,w_ref[h,BLOCK:PAIR],*mixs[h][1])
            s=jnp.concatenate([mm(qm_ref[h,0:BLOCK],st0,1,1),mm(qm_ref[h,BLOCK:PAIR],st1,1,1)],axis=0)
            s=jnp.where(ok,s*SCALE,-1e30)
            sbuf[h,c]=s
            hist_ref[0,0,h,rows,:]=st0
            hist_ref[0,1,h,rows,:]=st1
            stack[h,rows,:]=st2
            new.append(jnp.maximum(pk[h],jnp.max(s,axis=1,keepdims=True)))
        return tuple(new)
    peak=lax.fori_loop(lo,hi,step,peak)
    ed=[jnp.exp(sd[h]-peak[h]) for h in range(nh)]
    tot=tuple(jnp.sum(e,axis=1,keepdims=True) for e in ed)
    def step2(c,tt):
        new=[]
        for h in range(nh):
            e=jnp.exp(sbuf[h,c]-peak[h])
            sbuf[h,c]=e
            new.append(tt[h]+jnp.sum(e,axis=1,keepdims=True))
        return tuple(new)
    tot=lax.fori_loop(lo,hi,step2,tot)
    inv=[1.0/t for t in tot]
    grow=pl.ds(pl.multiple_of(g*PAIR,PAIR),PAIR)
    acc=tuple(mm((ed[h]*inv[h]).astype(bf16),v_ref[h,grow,:],1,0) for h in range(nh))
    def step3(c,ac):
        rows=pl.ds(pl.multiple_of(c*CHUNK,CHUNK),CHUNK)
        return tuple(ac[h]+mm((sbuf[h,c]*inv[h]).astype(bf16),v_ref[h,rows,:],1,0) for h in range(nh))
    acc=lax.fori_loop(lo,hi,step3,acc)
    for h in range(nh):
        out_ref[:,h*E_:(h+1)*E_]=acc[h].astype(bf16)
        lse_ref[h]=jnp.broadcast_to(peak[h]+jnp.log(tot[h]),(PAIR,E_))
        stack[h,grow,:]=kmf_ref[h]

def run_forward(ends,qm,kmf,w,mix,loc,v):
    nh,L,_=qm.shape; G=L//PAIR; docs=ends.shape[0]
    blk=pl.BlockSpec((nh,PAIR,E_),lambda g:(0,g,0))
    return pl.pallas_call(functools.partial(forward_kernel,nh,docs),
        grid=(G,),
        in_specs=[pl.BlockSpec(memory_space=pltpu.SMEM)]+[blk]*5+[pl.BlockSpec((nh,L,E_),lambda g:(0,0,0))],
        out_specs=[pl.BlockSpec((PAIR,nh*E_),lambda g:(g,0)),blk,pl.BlockSpec((1,2,nh,L,E_),lambda g:(g,0,0,0,0))],
        out_shape=[jax.ShapeDtypeStruct((L,nh*E_),bf16),jax.ShapeDtypeStruct((nh,L,E_),f32),jax.ShapeDtypeStruct((G,2,nh,L,E_),bf16)],
        scratch_shapes=[pltpu.VMEM((nh,L,E_),bf16),pltpu.VMEM((nh,-(-L//CHUNK),PAIR,CHUNK),f32)],
        cost_estimate=pl.CostEstimate(flops=nh*L*L*128*8,bytes_accessed=nh*L*128*24+G*nh*L*512,transcendentals=nh*L*L),
    )(ends,qm,kmf,w,mix,loc,v)

def backward_kernel(nh,docs,ngrp,ends_ref,qm_ref,w_ref,mix_ref,loc_ref,lse_ref,do_ref,hist_ref,v_ref,
                    dqm_ref,dloc_ref,dkf_ref,dw_ref,dmix_ref,dv_ref,grad,pbuf,dpbuf):
    g=ngrp-1-pl.program_id(0)
    @pl.when(g==ngrp-1)
    def _():
        grad[...]=jnp.zeros_like(grad)
        dv_ref[...]=jnp.zeros_like(dv_ref)
    lo,hi=chunk_range(ends_ref,docs,g)
    rowstart=start_of(ends_ref,docs,tile_pos(g,(PAIR,PAIR)))
    cc=lax.broadcasted_iota(jnp.int32,(PAIR,PAIR),1)
    rr=lax.broadcasted_iota(jnp.int32,(PAIR,PAIR),0)
    okd=(cc<=rr)&(cc+g*PAIR>=rowstart)
    start2=start_of(ends_ref,docs,tile_pos(g,(PAIR,CHUNK)))
    c2=lax.broadcasted_iota(jnp.int32,(PAIR,CHUNK),1)
    grow=pl.ds(pl.multiple_of(g*PAIR,PAIR),PAIR)
    do=[do_ref[:,h*E_:(h+1)*E_] for h in range(nh)]
    lse=[lse_ref[h,:,0:1] for h in range(nh)]
    pd=[jnp.exp(jnp.where(okd,loc_ref[h]*SCALE,-1e30)-lse[h]) for h in range(nh)]
    dpd=[mm(do[h],v_ref[h,grow,:],1,1) for h in range(nh)]
    delta=tuple(jnp.sum(pd[h]*dpd[h],axis=1,keepdims=True) for h in range(nh))
    def step(c,dl):
        rows=pl.ds(pl.multiple_of(c*CHUNK,CHUNK),CHUNK)
        ok=(c2+c*CHUNK>=start2)&(c2+c*CHUNK<g*PAIR)
        new=[]
        for h in range(nh):
            st0=hist_ref[0,0,h,rows,:]; st1=hist_ref[0,1,h,rows,:]
            s=jnp.concatenate([mm(qm_ref[h,0:BLOCK],st0,1,1),mm(qm_ref[h,BLOCK:PAIR],st1,1,1)],axis=0)
            p=jnp.exp(jnp.where(ok,s*SCALE,-1e30)-lse[h])
            dp=mm(do[h],v_ref[h,rows,:],1,1)
            pbuf[h,c]=p; dpbuf[h,c]=dp
            new.append(dl[h]+jnp.sum(p*dp,axis=1,keepdims=True))
        return tuple(new)
    delta=lax.fori_loop(lo,hi,step,delta)
    for h in range(nh):
        dloc_ref[h]=(pd[h]*(dpd[h]-delta[h])).astype(bf16)
        dv_ref[h,grow,:]=dv_ref[h,grow,:]+mm(pd[h].astype(bf16),do[h],0,0)
        dkf_ref[h]=grad[h,grow,:]
    mixs=[[halves(mix_ref[h,b*BLOCK:(b+1)*BLOCK]) for b in range(2)] for h in range(nh)]
    zero=jnp.zeros((BLOCK,E_),f32)
    def pull(gr,st,w,mh,ml,qm,ds):
        ph,pl_=halves(mm(st,w,1,1))
        gh,gl=halves(gr)
        u=mm(gh,mh,1,1)+(mm(gh,ml,1,1)+mm(gl,mh,1,1))
        uh,ul=halves(u)
        dw=mm(uh,st,0,0)+mm(ul,st,0,0)
        dm=mm(ph,gh,0,0)+(mm(ph,gl,0,0)+mm(pl_,gh,0,0))
        out=gr-(mm(uh,w,1,0)+mm(ul,w,1,0))+mm(ds,qm,0,0)*SCALE
        return out,dw,dm
    def step2(c,carry):
        rows=pl.ds(pl.multiple_of(c*CHUNK,CHUNK),CHUNK)
        new=[]
        for h in range(nh):
            dq0,dq1,dw0,dw1,dm0,dm1=carry[h]
            p=pbuf[h,c]
            ds=(p*(dpbuf[h,c]-delta[h])).astype(bf16)
            ds0=ds[0:BLOCK]; ds1=ds[BLOCK:PAIR]
            st0=hist_ref[0,0,h,rows,:]; st1=hist_ref[0,1,h,rows,:]
            dq0=dq0+mm(ds0,st0,1,0); dq1=dq1+mm(ds1,st1,1,0)
            dv_ref[h,rows,:]=dv_ref[h,rows,:]+mm(p.astype(bf16),do[h],0,0)
            gr=grad[h,rows,:]
            gr,a,b=pull(gr,st1,w_ref[h,BLOCK:PAIR],*mixs[h][1],qm_ref[h,BLOCK:PAIR],ds1)
            dw1=dw1-a; dm1=dm1-b
            gr,a,b=pull(gr,st0,w_ref[h,0:BLOCK],*mixs[h][0],qm_ref[h,0:BLOCK],ds0)
            dw0=dw0-a; dm0=dm0-b
            grad[h,rows,:]=gr
            new.append((dq0,dq1,dw0,dw1,dm0,dm1))
        return tuple(new)
    res=lax.fori_loop(lo,hi,step2,tuple((zero,)*6 for _ in range(nh)))
    for h in range(nh):
        dq0,dq1,dw0,dw1,dm0,dm1=res[h]
        dqm_ref[h,0:BLOCK]=dq0*SCALE; dqm_ref[h,BLOCK:PAIR]=dq1*SCALE
        dw_ref[h,0:BLOCK]=dw0; dw_ref[h,BLOCK:PAIR]=dw1
        dmix_ref[h,0:BLOCK]=dm0; dmix_ref[h,BLOCK:PAIR]=dm1

def run_backward(ends,qm,w,mix,loc,lse,do,hist,v):
    nh,L,_=qm.shape; G=L//PAIR; docs=ends.shape[0]
    blk=pl.BlockSpec((nh,PAIR,E_),lambda i:(0,G-1-i,0))
    o=lambda dt: jax.ShapeDtypeStruct((nh,L,E_),dt)
    full=pl.BlockSpec((nh,L,E_),lambda i:(0,0,0))
    return pl.pallas_call(functools.partial(backward_kernel,nh,docs,G),
        grid=(G,),
        in_specs=[pl.BlockSpec(memory_space=pltpu.SMEM)]+[blk]*5+[pl.BlockSpec((PAIR,nh*E_),lambda i:(G-1-i,0)),
                  pl.BlockSpec((1,2,nh,L,E_),lambda i:(G-1-i,0,0,0,0)),full],
        out_specs=[blk]*5+[full],
        out_shape=[o(f32),o(bf16),o(f32),o(f32),o(f32),o(f32)],
        scratch_shapes=[pltpu.VMEM((nh,L,E_),f32)]+[pltpu.VMEM((nh,-(-L//CHUNK),PAIR,CHUNK),f32)]*2,
        cost_estimate=pl.CostEstimate(flops=nh*L*L*128*20,bytes_accessed=nh*L*128*40+G*nh*L*512,transcendentals=nh*L*L),
    )(ends,qm,w,mix,loc,lse,do,hist,v)

def factor_back_kernel(nh,proj_ref,bias_ref,w_ref,qm_ref,kmp_ref,mix_ref,x_ref,
                       dqm_ref,dloc_ref,dkf_ref,dw_ref,dmix_ref,dv_ref,dproj_ref,dbias_ref):
    g=pl.program_id(0)
    r,c,same=pair_masks()
    eye=r==c
    lane=lax.broadcasted_iota(jnp.int32,(PAIR,E_),1)
    dlog_all=jnp.zeros((PAIR,E_),f32)
    for h in range(nh):
        q,k,hr,logit=head_inputs(proj_ref,slice(None),h,nh)
        beta=2.0*jax.nn.sigmoid(logit+bias_ref[h])
        rs=lax.rsqrt(jnp.sum(hr*hr,axis=1,keepdims=True)+EPS)
        w=w_ref[h]; qm=qm_ref[h]; kmp=kmp_ref[h]; mix=mix_ref[h]; x=x_ref[h]
        t,xq,y,xt,ty=factors_of(q,k,w,beta,x,r,c,same)
        ds=dloc_ref[h]
        dsl=jnp.where(same,ds.astype(f32),0.0).astype(bf16)
        dsc=jnp.where(same,0.0,ds.astype(f32)).astype(bf16)
        gk=dkf_ref[h]
        p=jnp.where((r<BLOCK)&(c>=BLOCK),mm(kmp,w,1,1),0.0)
        u=jnp.where((r<BLOCK)&(c>=BLOCK),mm_xy(gk,mix,1,1),0.0)
        dkm=gk-mm_x(u,w,1,0)+mm(dsc,qm,0,0)*SCALE
        dw=dw_ref[h]-mm_x(u,kmp,0,0)
        dmix=dmix_ref[h]-mm_xy(p,gk,0,0)
        dqm=dqm_ref[h]+mm(dsc,kmp,1,0)*SCALE
        dxt=-(mm_y(dsl,y,1,1)*SCALE)-mm_x(dqm,w,1,1)
        dty=-mm_y(w,dkm,1,1)
        dy=-(mm_x(xt,dsl,0,0)*SCALE)+mm_xy(t,dty,0,0)
        dy=jnp.where(same&(r>c),dy,0.0)
        dxt=jnp.where(same,dxt,0.0); dty=jnp.where(same,dty,0.0)
        dt=mm_xy(xq,dxt,0,0)+mm_xy(dty,y,1,1)+mm_y(w,dmix,1,1)
        dt=jnp.where(same,dt,0.0)
        dxq=jnp.where(same&(r>=c),mm_xy(dxt,t,1,1),0.0)
        dw=dw-mm_xy(xt,dqm,0,0)-mm_xy(ty,dkm,1,0)+mm_xy(t,dmix,1,0)+mm_x(dxq,q,0,0)+mm_x(dy,k,1,0)
        dq=dqm+mm(dsl,k,1,0)*SCALE+mm_x(dxq,w,1,0)
        dk=dkm+mm(dsl,q,0,0)*SCALE+mm_x(dy,w,0,0)
        dx=dt*col_to_row(beta,eye)
        dbr=jnp.sum(dt*x,axis=0,keepdims=True)
        da=jnp.where(same&(r>c),-mm_xy(mm_xy(x,dx,0,0),x,1,1),0.0)
        gram=mm(w,w,1,1)
        dbeta=jnp.sum(da*gram,axis=1,keepdims=True)+jnp.sum(jnp.where(eye,dbr,0.0),axis=1,keepdims=True)
        dg=beta*da
        dw=dw+mm_x(dg,w,1,0)+mm_x(dg,w,0,0)
        dlog=dbeta*beta*(1.0-0.5*beta)
        dhr=rs*dw-(rs*rs*rs)*hr*jnp.sum(hr*dw,axis=1,keepdims=True)
        dproj_ref[:,h*E_:(h+1)*E_]=dq.astype(bf16)
        dproj_ref[:,(nh+h)*E_:(nh+h+1)*E_]=dk.astype(bf16)
        dproj_ref[:,(2*nh+h)*E_:(2*nh+h+1)*E_]=dv_ref[h].astype(bf16)
        dproj_ref[:,(3*nh+h)*E_:(3*nh+h+1)*E_]=dhr.astype(bf16)
        dlog_all=dlog_all+jnp.where(lane==h,dlog,0.0)
    dproj_ref[:,4*nh*E_:(4*nh+1)*E_]=dlog_all.astype(bf16)
    @pl.when(g==0)
    def _():
        dbias_ref[...]=jnp.zeros_like(dbias_ref)
    dbias_ref[...]=dbias_ref[...]+jnp.sum(dlog_all,axis=0,keepdims=True)

def run_factor_back(proj,bias,w,qm,kmp,mix,x,dqm,dloc,dkf,dw,dmix,dv):
    nh,L,_=qm.shape; wd=proj.shape[1]
    blk=pl.BlockSpec((nh,PAIR,E_),lambda g:(0,g,0))
    return pl.pallas_call(functools.partial(factor_back_kernel,nh),
        grid=(L//PAIR,),
        in_specs=[pl.BlockSpec((PAIR,wd),lambda g:(g,0)),pl.BlockSpec(memory_space=pltpu.SMEM)]+[blk]*11,
        out_specs=[pl.BlockSpec((PAIR,wd),lambda g:(g,0)),pl.BlockSpec((1,E_),lambda g:(0,0))],
        out_shape=[jax.ShapeDtypeStruct((L,wd),bf16),jax.ShapeDtypeStruct((1,E_),f32)],
        cost_estimate=pl.CostEstimate(flops=L//PAIR*nh*100*2*128**3,bytes_accessed=L*wd*6+nh*L*128*40,transcendentals=0),
    )(proj,bias,w,qm,kmp,mix,x,dqm,dloc,dkf,dw,dmix,dv)


from jax.sharding import Mesh, PartitionSpec as P

HEADS = 12
DP = ("x", "core")
SEQ = ("hi", "lo")
TP = ("x", "core", "lo")
ALL = ("x", "core", "hi", "lo")


def rms_scale(values):
    return lax.rsqrt(jnp.mean(values * values, axis=-1, keepdims=True) + EPS)


def rms_back(grad, values, scale, gains):
    scaled = grad * gains
    inner = jnp.mean(scaled * values, axis=-1, keepdims=True)
    return scale * scaled - (scale * scale * scale) * values * inner


def dot(a, b):
    return jnp.dot(a, b, preferred_element_type=f32)


def dot_nt(a, b):
    return lax.dot_general(a, b, (((1,), (1,)), ((), ())), preferred_element_type=f32)


def dot_tn(a, b):
    return lax.dot_general(a, b, (((0,), (0,)), ((), ())), preferred_element_type=f32)


def gather(shard, axes):
    return lax.all_gather(shard, axes, axis=0, tiled=True)


def scatter(full, axes):
    return lax.psum_scatter(full, axes, scatter_dimension=0, tiled=True)


def exchange(pieces, axes):
    return lax.all_to_all(pieces, axes, 0, 0, tiled=True)


def on_device(inputs, doc_lengths, w_query, w_key, w_value, w_house, w_beta, beta_bias, norm_attn, w_out,
              norm_mlp, w_gate, w_up, w_down, grad_y):
    hi_n, lo_n = lax.axis_size("hi"), lax.axis_size("lo")
    dp_n = lax.axis_size("x") * lax.axis_size("core")
    seq_n = hi_n * lo_n
    tp_n = dp_n * lo_n
    seq_at = lax.axis_index("hi") * lo_n + lax.axis_index("lo")
    dp_at = lax.axis_index("x") * lax.axis_size("core") + lax.axis_index("core")
    rows, width = w_query.shape
    tokens = inputs.shape[1]
    length = tokens * seq_n
    ff_rows = w_down.shape[0]
    ff_n = ff_rows * hi_n
    nh = -(-HEADS // seq_n)
    head_cols = nh * E_
    slot = 4 * head_cols + E_
    x_own = inputs[0]
    gy_own = grad_y[0]

    def slots(w, each):
        return jnp.pad(w, ((0, 0), (0, seq_n * each - w.shape[1]))).reshape(rows, seq_n, each)

    spare = jnp.concatenate([
        slots(w_beta, nh),
        jnp.broadcast_to(jnp.stack([norm_attn, norm_mlp], -1)[:, None], (rows, seq_n, 2)),
        jnp.zeros((rows, seq_n, E_ - nh - 2), bf16)], axis=2)
    pack = jnp.concatenate([slots(w, head_cols) for w in (w_query, w_key, w_value, w_house)] + [spare], axis=2)
    x_row = gather(x_own, SEQ)
    pack = exchange(jnp.swapaxes(pack, 0, 1), SEQ)
    pack = gather(pack, DP).reshape(width, slot)
    gains = pack[:, 4 * head_cols + nh:4 * head_cols + nh + 2].astype(f32)
    gain_one, gain_two = gains[:, 0][None], gains[:, 1][None]
    out_full = gather(w_out, ALL)

    def unit_pieces(w):
        w = w.reshape(rows, dp_n, hi_n, lo_n, ff_rows)
        return jnp.transpose(w, (1, 3, 0, 2, 4)).reshape(tp_n, rows, ff_n)

    gate_up = exchange(jnp.concatenate([unit_pieces(w_gate), unit_pieces(w_up)], axis=2), TP)
    gate_up = gather(gate_up, "hi").reshape(width, 2 * ff_n)
    down = gather(w_down, "hi")
    gy_all = gather(gy_own, TP)

    x_rowf = x_row.astype(f32)
    row_scale = rms_scale(x_rowf)
    normed = (x_rowf * row_scale * gain_one).astype(bf16)
    proj = dot(normed, pack)
    bias_own = lax.dynamic_slice_in_dim(jnp.pad(beta_bias, (0, seq_n * nh - HEADS)), seq_at * nh, nh)
    ends = jnp.cumsum(doc_lengths[0])
    values = jnp.swapaxes(proj[:, 2 * head_cols:3 * head_cols].astype(bf16).reshape(length, nh, E_), 0, 1)
    houses, moved_q, moved_k, final_k, mixing, local_raw, inverse = run_factors(proj, bias_own, nh)
    mixed, log_sum, history = run_forward(ends, moved_q, final_k, houses, mixing, local_raw, values)
    mixed = exchange(mixed.reshape(seq_n, tokens, head_cols), SEQ)
    mixed = jnp.swapaxes(mixed, 0, 1).reshape(tokens, seq_n * head_cols)[:, :width]

    x_float = x_own.astype(f32)
    middle = x_float + dot(mixed, out_full)
    mid_scale = rms_scale(middle)
    normed_mlp = (middle * mid_scale * gain_two).astype(bf16)

    def to_owner_order(a):
        return jnp.swapaxes(a.reshape(tokens, dp_n, hi_n, lo_n * rows), 1, 2).reshape(tokens, width)

    def from_owner_order(a):
        return jnp.swapaxes(a.reshape(tokens, hi_n, dp_n, lo_n * rows), 1, 2).reshape(tokens, width)

    nm_all = gather(to_owner_order(normed_mlp), TP)
    both = dot(nm_all, gate_up)
    gate_val, up_val = both[:, :ff_n], both[:, ff_n:]
    sig = jax.nn.sigmoid(gate_val)
    silu = gate_val * sig
    hidden = (silu * up_val).astype(bf16)
    result = middle + scatter(dot(hidden, down).astype(bf16), TP).astype(f32)

    d_hidden = dot_nt(gy_all, down)
    d_gate = d_hidden * up_val * (sig * (1.0 + gate_val * (1.0 - sig)))
    d_up = d_hidden * silu
    d_both = jnp.concatenate([d_gate.astype(bf16), d_up.astype(bf16)], axis=1)
    d_nm = from_owner_order(scatter(dot_nt(d_both, gate_up).astype(bf16), TP)).astype(f32)
    grad_both = dot_tn(nm_all, d_both).astype(bf16)
    grad_down = dot_tn(hidden, gy_all).astype(bf16)
    grad_down = scatter(grad_down, "hi").astype(f32)
    grad_both = scatter(grad_both.reshape(hi_n * tp_n, rows, 2 * ff_n), "hi")
    d_middle = gy_own.astype(f32) + rms_back(d_nm, middle, mid_scale, gain_two)
    gain_mlp_part = jnp.sum(d_nm * middle * mid_scale, axis=0)

    d_branch = d_middle.astype(bf16)
    d_mixed = dot_nt(d_branch, out_full).astype(bf16)
    grad_out = scatter(dot_tn(mixed, d_branch).astype(bf16), ALL).astype(f32)
    d_mixed = jnp.pad(d_mixed, ((0, 0), (0, seq_n * head_cols - width))).reshape(tokens, seq_n, head_cols)
    d_mixed = exchange(jnp.swapaxes(d_mixed, 0, 1), SEQ).reshape(length, head_cols)
    d_mq, d_local, d_fk, d_w, d_mix, d_val = run_backward(
        ends, moved_q, houses, mixing, local_raw, log_sum, d_mixed, history, values)
    d_proj, d_bias = run_factor_back(proj, bias_own, houses, moved_q, moved_k, mixing, inverse,
                                     d_mq, d_local, d_fk, d_w, d_mix, d_val)
    d_normed_part = dot_nt(d_proj, pack)
    d_normed = scatter(d_normed_part.astype(bf16), SEQ).astype(f32)
    gain_attn_part = jnp.sum(d_normed_part * (x_rowf * row_scale), axis=0)
    grad_x = d_middle + rms_back(d_normed, x_float, rms_scale(x_float), gain_one)

    grad_both = exchange(grad_both, TP)
    grad_both = grad_both.reshape(dp_n, lo_n, rows, 2, hi_n, ff_rows)
    grad_both = jnp.transpose(grad_both, (3, 2, 0, 4, 1, 5)).reshape(2, rows, -1).astype(f32)

    grad_pack = dot_tn(normed, d_proj)
    lane = jnp.arange(E_)[None]
    spare_grad = grad_pack[:, 4 * head_cols:]
    own = nh + dp_at
    spare_grad = jnp.where(lane == own, gain_attn_part[:, None], spare_grad)
    spare_grad = jnp.where(lane == own + dp_n, gain_mlp_part[:, None], spare_grad)
    base = nh + 2 * dp_n
    for h in range(nh):
        high = d_bias[0, h].astype(bf16).astype(f32)
        at = base + (dp_at * nh + h) * 2
        spare_grad = jnp.where(lane == at, high, spare_grad)
        spare_grad = jnp.where(lane == at + 1, d_bias[0, h] - high, spare_grad)
    grad_pack = jnp.concatenate([grad_pack[:, :4 * head_cols], spare_grad], axis=1).astype(bf16)
    grad_pack = exchange(scatter(grad_pack, DP).reshape(seq_n, rows, slot), SEQ).astype(f32)

    def whole(part, n):
        return jnp.swapaxes(part, 0, 1).reshape(rows, -1)[:, :n]

    grads = [whole(grad_pack[:, :, i * head_cols:(i + 1) * head_cols], width) for i in range(4)]
    spare_grad = grad_pack[:, :, 4 * head_cols:]
    grad_beta = whole(spare_grad[:, :, :nh], HEADS)
    grad_gain_attn = jnp.sum(spare_grad[:, :, nh:nh + dp_n], axis=(0, 2))
    grad_gain_mlp = jnp.sum(spare_grad[:, :, nh + dp_n:base], axis=(0, 2))
    bias_parts = spare_grad[:, 0, base:base + 2 * nh * dp_n].reshape(seq_n, dp_n, nh, 2)
    grad_bias = jnp.sum(bias_parts, axis=(1, 3)).reshape(-1)[:HEADS]
    return (
        result.astype(bf16)[None],
        grad_x[None],
        grads[0],
        grads[1],
        grads[2],
        grads[3],
        grad_beta,
        grad_bias,
        grad_gain_attn,
        grad_out,
        grad_gain_mlp,
        grad_both[0],
        grad_both[1],
        grad_down,
    )


def solution(mesh):
    dp_n, seq_n = mesh.devices.shape
    fine = Mesh(mesh.devices.reshape(dp_n // 2, 2, seq_n // 2, 2), ALL)
    by_rows, tokens = P(ALL, None), P(DP, SEQ, None)
    in_specs = (tokens, P(DP, None), by_rows, by_rows, by_rows, by_rows, by_rows, P(), P(ALL), by_rows, P(ALL),
                by_rows, by_rows, by_rows, tokens)
    out_specs = (tokens, tokens, by_rows, by_rows, by_rows, by_rows, by_rows, P(), P(ALL), by_rows, P(ALL),
                 by_rows, by_rows, by_rows)
    return jax.shard_map(on_device, mesh=fine, in_specs=in_specs, out_specs=out_specs, check_vma=False)
```

```python
import functools
import jax, jax.numpy as jnp
from jax import lax
from jax.experimental import pallas as pl
from jax.experimental.pallas import tpu as pltpu

bf16=jnp.bfloat16; f32=jnp.float32
E_=128; BLOCK=64; PAIR=128; CHUNK=256
EPS=1e-6
SCALE=128**-0.5

def spent(us):
    return pl.CostEstimate(flops=int(us*1.1e9),bytes_accessed=1<<20,transcendentals=0)
def mm(a,b,ca,cb):
    return lax.dot_general(a,b,(((ca,),(cb,)),((),())),preferred_element_type=f32)
def halves(a):
    hi=a.astype(bf16)
    return hi,(a-hi.astype(f32)).astype(bf16)
def mm_x(a,b,ca,cb):
    h,l=halves(a)
    return mm(h,b,ca,cb)+mm(l,b,ca,cb)
def mm_y(a,b,ca,cb):
    h,l=halves(b)
    return mm(a,h,ca,cb)+mm(a,l,ca,cb)
def mm_xy(a,b,ca,cb):
    ah,al=halves(a); bh,bl=halves(b)
    return mm(ah,bh,ca,cb)+(mm(ah,bl,ca,cb)+mm(al,bh,ca,cb))

def pair_masks():
    r=lax.broadcasted_iota(jnp.int32,(PAIR,PAIR),0)
    c=lax.broadcasted_iota(jnp.int32,(PAIR,PAIR),1)
    same=(r//BLOCK)==(c//BLOCK)
    return r,c,same

def col_to_row(col,eye):
    return jnp.sum(jnp.where(eye,col,0.0),axis=0,keepdims=True)

def inverse_of(a,r,c):
    eye=(r==c).astype(f32)
    x=eye-jnp.where((r//2)==(c//2),a,0.0)
    size=2
    while size<BLOCK:
        part=jnp.where(((r//(2*size))==(c//(2*size)))&((r//size)!=(c//size)),a,0.0)
        x=x-mm_xy(mm_xy(x,part,1,0),x,1,0)
        size*=2
    return x

def factors_of(q,k,w,beta,x,r,c,same):
    eye=r==c
    t=x*col_to_row(beta,eye)
    xq=jnp.where(same&(r>=c),mm(q,w,1,1),0.0)
    y=jnp.where(same&(r>c),mm(w,k,1,1),0.0)
    xt=mm_xy(xq,t,1,0)
    ty=mm_xy(t,y,1,0)
    return t,xq,y,xt,ty

def head_inputs(proj_ref,rows,h,nh):
    q=proj_ref[rows,h*E_:(h+1)*E_].astype(bf16)
    k=proj_ref[rows,(nh+h)*E_:(nh+h+1)*E_].astype(bf16)
    hr=proj_ref[rows,(3*nh+h)*E_:(3*nh+h+1)*E_]
    ex=proj_ref[rows,4*nh*E_:(4*nh+1)*E_]
    lane=lax.broadcasted_iota(jnp.int32,ex.shape,1)
    logit=jnp.sum(jnp.where(lane==h,ex,0.0),axis=1,keepdims=True)
    return q,k,hr,logit

def factor_kernel(nh,proj_ref,bias_ref,w_ref,qm_ref,kmp_ref,kmf_ref,mix_ref,loc_ref,x_ref):
    r,c,same=pair_masks()
    for h in range(nh):
        q,k,hr,logit=head_inputs(proj_ref,slice(None),h,nh)
        beta=2.0*jax.nn.sigmoid(logit+bias_ref[h])
        w=(hr*lax.rsqrt(jnp.sum(hr*hr,axis=1,keepdims=True)+EPS)).astype(bf16)
        a=jnp.where(same&(r>c),beta*mm(w,w,1,1),0.0)
        x=inverse_of(a,r,c)
        t,xq,y,xt,ty=factors_of(q,k,w,beta,x,r,c,same)
        qm=(q.astype(f32)-mm_x(xt,w,1,0)).astype(bf16)
        kmp=(k.astype(f32)-mm_x(ty,w,0,0)).astype(bf16)
        mix=mm_x(t,w,0,0)
        inner=mm(q,k,1,1)-mm_xy(xt,y,1,0)
        cross=mm(qm,kmp,1,1)
        loc=jnp.where(same,inner,cross)
        p=jnp.where((r<BLOCK)&(c>=BLOCK),mm(kmp,w,1,1),0.0)
        kmf=(kmp.astype(f32)-mm_xy(p,mix,1,0)).astype(bf16)
        w_ref[h]=w; qm_ref[h]=qm; kmp_ref[h]=kmp; kmf_ref[h]=kmf
        mix_ref[h]=mix; loc_ref[h]=loc; x_ref[h]=x

def run_factors(proj,bias,nh):
    L=proj.shape[0]; wd=proj.shape[1]
    blk=pl.BlockSpec((nh,PAIR,E_),lambda g:(0,g,0))
    o=lambda dt: jax.ShapeDtypeStruct((nh,L,E_),dt)
    return pl.pallas_call(functools.partial(factor_kernel,nh),
        grid=(L//PAIR,),
        in_specs=[pl.BlockSpec((PAIR,wd),lambda g:(g,0)),pl.BlockSpec(memory_space=pltpu.SMEM)],
        out_specs=[blk]*7,
        out_shape=[o(bf16),o(bf16),o(bf16),o(bf16),o(f32),o(f32),o(f32)],
        cost_estimate=spent(38),
    )(proj,bias)

def start_of(ends_ref,docs,pos):
    s=jnp.zeros_like(pos)
    for d in range(docs):
        s=jnp.maximum(s,jnp.where(pos>=ends_ref[d],ends_ref[d],0))
    return s

def scalar_start(ends_ref,docs,pos):
    s=jnp.int32(0)
    for d in range(docs):
        s=jnp.maximum(s,jnp.where(pos>=ends_ref[d],ends_ref[d],0))
    return s

def tile_pos(g,shape):
    return g*PAIR+lax.broadcasted_iota(jnp.int32,shape,0)

def chunk_range(ends_ref,docs,g):
    lo=scalar_start(ends_ref,docs,g*PAIR)//CHUNK
    hi=(g*PAIR+CHUNK-1)//CHUNK
    return lo,hi

def carried_forward(st,w,mh,ml):
    ph,pl_=halves(mm(st,w,1,1))
    return (st.astype(f32)-(mm(ph,mh,1,0)+(mm(ph,ml,1,0)+mm(pl_,mh,1,0)))).astype(bf16)

def forward_kernel(nh,docs,ends_ref,qm_ref,kmf_ref,w_ref,mix_ref,loc_ref,v_ref,
                   out_ref,lse_ref,hist_ref,stack,sbuf):
    g=pl.program_id(0)
    @pl.when(g==0)
    def _():
        stack[...]=jnp.zeros_like(stack)
    lo,hi=chunk_range(ends_ref,docs,g)
    rowstart=start_of(ends_ref,docs,tile_pos(g,(PAIR,PAIR)))
    cc=lax.broadcasted_iota(jnp.int32,(PAIR,PAIR),1)
    rr=lax.broadcasted_iota(jnp.int32,(PAIR,PAIR),0)
    okd=(cc<=rr)&(cc+g*PAIR>=rowstart)
    sd=[jnp.where(okd,loc_ref[h]*SCALE,-1e30) for h in range(nh)]
    peak=tuple(jnp.max(s,axis=1,keepdims=True) for s in sd)
    start2=start_of(ends_ref,docs,tile_pos(g,(PAIR,CHUNK)))
    c2=lax.broadcasted_iota(jnp.int32,(PAIR,CHUNK),1)
    mixs=[[halves(mix_ref[h,b*BLOCK:(b+1)*BLOCK]) for b in range(2)] for h in range(nh)]
    def step(c,pk):
        rows=pl.ds(pl.multiple_of(c*CHUNK,CHUNK),CHUNK)
        ok=(c2+c*CHUNK>=start2)&(c2+c*CHUNK<g*PAIR)
        new=[]
        for h in range(nh):
            st0=stack[h,rows,:]
            st1=carried_forward(st0,w_ref[h,0:BLOCK],*mixs[h][0])
            st2=carried_forward(st1,w_ref[h,BLOCK:PAIR],*mixs[h][1])
            s=jnp.concatenate([mm(qm_ref[h,0:BLOCK],st0,1,1),mm(qm_ref[h,BLOCK:PAIR],st1,1,1)],axis=0)
            s=jnp.where(ok,s*SCALE,-1e30)
            sbuf[h,c]=s
            hist_ref[0,0,h,rows,:]=st0
            hist_ref[0,1,h,rows,:]=st1
            stack[h,rows,:]=st2
            new.append(jnp.maximum(pk[h],jnp.max(s,axis=1,keepdims=True)))
        return tuple(new)
    peak=lax.fori_loop(lo,hi,step,peak)
    ed=[jnp.exp(sd[h]-peak[h]) for h in range(nh)]
    tot=tuple(jnp.sum(e,axis=1,keepdims=True) for e in ed)
    def step2(c,tt):
        new=[]
        for h in range(nh):
            e=jnp.exp(sbuf[h,c]-peak[h])
            sbuf[h,c]=e
            new.append(tt[h]+jnp.sum(e,axis=1,keepdims=True))
        return tuple(new)
    tot=lax.fori_loop(lo,hi,step2,tot)
    inv=[1.0/t for t in tot]
    grow=pl.ds(pl.multiple_of(g*PAIR,PAIR),PAIR)
    acc=tuple(mm((ed[h]*inv[h]).astype(bf16),v_ref[h,grow,:],1,0) for h in range(nh))
    def step3(c,ac):
        rows=pl.ds(pl.multiple_of(c*CHUNK,CHUNK),CHUNK)
        return tuple(ac[h]+mm((sbuf[h,c]*inv[h]).astype(bf16),v_ref[h,rows,:],1,0) for h in range(nh))
    acc=lax.fori_loop(lo,hi,step3,acc)
    for h in range(nh):
        out_ref[:,h*E_:(h+1)*E_]=acc[h].astype(bf16)
        lse_ref[h]=jnp.broadcast_to(peak[h]+jnp.log(tot[h]),(PAIR,E_))
        stack[h,grow,:]=kmf_ref[h]

def run_forward(ends,qm,kmf,w,mix,loc,v):
    nh,L,_=qm.shape; G=L//PAIR; docs=ends.shape[0]
    blk=pl.BlockSpec((nh,PAIR,E_),lambda g:(0,g,0))
    return pl.pallas_call(functools.partial(forward_kernel,nh,docs),
        grid=(G,),
        in_specs=[pl.BlockSpec(memory_space=pltpu.SMEM)]+[blk]*5+[pl.BlockSpec((nh,L,E_),lambda g:(0,0,0))],
        out_specs=[pl.BlockSpec((PAIR,nh*E_),lambda g:(g,0)),blk,pl.BlockSpec((1,2,nh,L,E_),lambda g:(g,0,0,0,0))],
        out_shape=[jax.ShapeDtypeStruct((L,nh*E_),bf16),jax.ShapeDtypeStruct((nh,L,E_),f32),jax.ShapeDtypeStruct((G,2,nh,L,E_),bf16)],
        scratch_shapes=[pltpu.VMEM((nh,L,E_),bf16),pltpu.VMEM((nh,-(-L//CHUNK),PAIR,CHUNK),f32)],
        cost_estimate=spent(22),
    )(ends,qm,kmf,w,mix,loc,v)

def backward_kernel(nh,docs,ngrp,ends_ref,qm_ref,w_ref,mix_ref,loc_ref,lse_ref,do_ref,hist_ref,v_ref,
                    dqm_ref,dloc_ref,dkf_ref,dw_ref,dmix_ref,dv_ref,grad,pbuf,dpbuf):
    g=ngrp-1-pl.program_id(0)
    @pl.when(g==ngrp-1)
    def _():
        grad[...]=jnp.zeros_like(grad)
        dv_ref[...]=jnp.zeros_like(dv_ref)
    lo,hi=chunk_range(ends_ref,docs,g)
    rowstart=start_of(ends_ref,docs,tile_pos(g,(PAIR,PAIR)))
    cc=lax.broadcasted_iota(jnp.int32,(PAIR,PAIR),1)
    rr=lax.broadcasted_iota(jnp.int32,(PAIR,PAIR),0)
    okd=(cc<=rr)&(cc+g*PAIR>=rowstart)
    start2=start_of(ends_ref,docs,tile_pos(g,(PAIR,CHUNK)))
    c2=lax.broadcasted_iota(jnp.int32,(PAIR,CHUNK),1)
    grow=pl.ds(pl.multiple_of(g*PAIR,PAIR),PAIR)
    do=[do_ref[:,h*E_:(h+1)*E_] for h in range(nh)]
    lse=[lse_ref[h,:,0:1] for h in range(nh)]
    pd=[jnp.exp(jnp.where(okd,loc_ref[h]*SCALE,-1e30)-lse[h]) for h in range(nh)]
    dpd=[mm(do[h],v_ref[h,grow,:],1,1) for h in range(nh)]
    delta=tuple(jnp.sum(pd[h]*dpd[h],axis=1,keepdims=True) for h in range(nh))
    def step(c,dl):
        rows=pl.ds(pl.multiple_of(c*CHUNK,CHUNK),CHUNK)
        ok=(c2+c*CHUNK>=start2)&(c2+c*CHUNK<g*PAIR)
        new=[]
        for h in range(nh):
            st0=hist_ref[0,0,h,rows,:]; st1=hist_ref[0,1,h,rows,:]
            s=jnp.concatenate([mm(qm_ref[h,0:BLOCK],st0,1,1),mm(qm_ref[h,BLOCK:PAIR],st1,1,1)],axis=0)
            p=jnp.exp(jnp.where(ok,s*SCALE,-1e30)-lse[h])
            dp=mm(do[h],v_ref[h,rows,:],1,1)
            pbuf[h,c]=p; dpbuf[h,c]=dp
            new.append(dl[h]+jnp.sum(p*dp,axis=1,keepdims=True))
        return tuple(new)
    delta=lax.fori_loop(lo,hi,step,delta)
    for h in range(nh):
        dloc_ref[h]=(pd[h]*(dpd[h]-delta[h])).astype(bf16)
        dv_ref[h,grow,:]=dv_ref[h,grow,:]+mm(pd[h].astype(bf16),do[h],0,0)
        dkf_ref[h]=grad[h,grow,:]
    mixs=[[halves(mix_ref[h,b*BLOCK:(b+1)*BLOCK]) for b in range(2)] for h in range(nh)]
    zero=jnp.zeros((BLOCK,E_),f32)
    def pull(gr,st,w,mh,ml,qm,ds):
        ph,pl_=halves(mm(st,w,1,1))
        gh,gl=halves(gr)
        u=mm(gh,mh,1,1)+(mm(gh,ml,1,1)+mm(gl,mh,1,1))
        uh,ul=halves(u)
        dw=mm(uh,st,0,0)+mm(ul,st,0,0)
        dm=mm(ph,gh,0,0)+(mm(ph,gl,0,0)+mm(pl_,gh,0,0))
        out=gr-(mm(uh,w,1,0)+mm(ul,w,1,0))+mm(ds,qm,0,0)*SCALE
        return out,dw,dm
    def step2(c,carry):
        rows=pl.ds(pl.multiple_of(c*CHUNK,CHUNK),CHUNK)
        new=[]
        for h in range(nh):
            dq0,dq1,dw0,dw1,dm0,dm1=carry[h]
            p=pbuf[h,c]
            ds=(p*(dpbuf[h,c]-delta[h])).astype(bf16)
            ds0=ds[0:BLOCK]; ds1=ds[BLOCK:PAIR]
            st0=hist_ref[0,0,h,rows,:]; st1=hist_ref[0,1,h,rows,:]
            dq0=dq0+mm(ds0,st0,1,0); dq1=dq1+mm(ds1,st1,1,0)
            dv_ref[h,rows,:]=dv_ref[h,rows,:]+mm(p.astype(bf16),do[h],0,0)
            gr=grad[h,rows,:]
            gr,a,b=pull(gr,st1,w_ref[h,BLOCK:PAIR],*mixs[h][1],qm_ref[h,BLOCK:PAIR],ds1)
            dw1=dw1-a; dm1=dm1-b
            gr,a,b=pull(gr,st0,w_ref[h,0:BLOCK],*mixs[h][0],qm_ref[h,0:BLOCK],ds0)
            dw0=dw0-a; dm0=dm0-b
            grad[h,rows,:]=gr
            new.append((dq0,dq1,dw0,dw1,dm0,dm1))
        return tuple(new)
    res=lax.fori_loop(lo,hi,step2,tuple((zero,)*6 for _ in range(nh)))
    for h in range(nh):
        dq0,dq1,dw0,dw1,dm0,dm1=res[h]
        dqm_ref[h,0:BLOCK]=dq0*SCALE; dqm_ref[h,BLOCK:PAIR]=dq1*SCALE
        dw_ref[h,0:BLOCK]=dw0; dw_ref[h,BLOCK:PAIR]=dw1
        dmix_ref[h,0:BLOCK]=dm0; dmix_ref[h,BLOCK:PAIR]=dm1

def run_backward(ends,qm,w,mix,loc,lse,do,hist,v):
    nh,L,_=qm.shape; G=L//PAIR; docs=ends.shape[0]
    blk=pl.BlockSpec((nh,PAIR,E_),lambda i:(0,G-1-i,0))
    o=lambda dt: jax.ShapeDtypeStruct((nh,L,E_),dt)
    full=pl.BlockSpec((nh,L,E_),lambda i:(0,0,0))
    return pl.pallas_call(functools.partial(backward_kernel,nh,docs,G),
        grid=(G,),
        in_specs=[pl.BlockSpec(memory_space=pltpu.SMEM)]+[blk]*5+[pl.BlockSpec((PAIR,nh*E_),lambda i:(G-1-i,0)),
                  pl.BlockSpec((1,2,nh,L,E_),lambda i:(G-1-i,0,0,0,0)),full],
        out_specs=[blk]*5+[full],
        out_shape=[o(f32),o(bf16),o(f32),o(f32),o(f32),o(f32)],
        scratch_shapes=[pltpu.VMEM((nh,L,E_),f32)]+[pltpu.VMEM((nh,-(-L//CHUNK),PAIR,CHUNK),f32)]*2,
        cost_estimate=spent(35),
    )(ends,qm,w,mix,loc,lse,do,hist,v)

def factor_back_kernel(nh,proj_ref,bias_ref,w_ref,qm_ref,kmp_ref,mix_ref,x_ref,
                       dqm_ref,dloc_ref,dkf_ref,dw_ref,dmix_ref,dv_ref,dproj_ref,dbias_ref):
    g=pl.program_id(0)
    r,c,same=pair_masks()
    eye=r==c
    lane=lax.broadcasted_iota(jnp.int32,(PAIR,E_),1)
    dlog_all=jnp.zeros((PAIR,E_),f32)
    for h in range(nh):
        q,k,hr,logit=head_inputs(proj_ref,slice(None),h,nh)
        beta=2.0*jax.nn.sigmoid(logit+bias_ref[h])
        rs=lax.rsqrt(jnp.sum(hr*hr,axis=1,keepdims=True)+EPS)
        w=w_ref[h]; qm=qm_ref[h]; kmp=kmp_ref[h]; mix=mix_ref[h]; x=x_ref[h]
        t,xq,y,xt,ty=factors_of(q,k,w,beta,x,r,c,same)
        ds=dloc_ref[h]
        dsl=jnp.where(same,ds.astype(f32),0.0).astype(bf16)
        dsc=jnp.where(same,0.0,ds.astype(f32)).astype(bf16)
        gk=dkf_ref[h]
        p=jnp.where((r<BLOCK)&(c>=BLOCK),mm(kmp,w,1,1),0.0)
        u=jnp.where((r<BLOCK)&(c>=BLOCK),mm_xy(gk,mix,1,1),0.0)
        dkm=gk-mm_x(u,w,1,0)+mm(dsc,qm,0,0)*SCALE
        dw=dw_ref[h]-mm_x(u,kmp,0,0)
        dmix=dmix_ref[h]-mm_xy(p,gk,0,0)
        dqm=dqm_ref[h]+mm(dsc,kmp,1,0)*SCALE
        dxt=-(mm_y(dsl,y,1,1)*SCALE)-mm_x(dqm,w,1,1)
        dty=-mm_y(w,dkm,1,1)
        dy=-(mm_x(xt,dsl,0,0)*SCALE)+mm_xy(t,dty,0,0)
        dy=jnp.where(same&(r>c),dy,0.0)
        dxt=jnp.where(same,dxt,0.0); dty=jnp.where(same,dty,0.0)
        dt=mm_xy(xq,dxt,0,0)+mm_xy(dty,y,1,1)+mm_y(w,dmix,1,1)
        dt=jnp.where(same,dt,0.0)
        dxq=jnp.where(same&(r>=c),mm_xy(dxt,t,1,1),0.0)
        dw=dw-mm_xy(xt,dqm,0,0)-mm_xy(ty,dkm,1,0)+mm_xy(t,dmix,1,0)+mm_x(dxq,q,0,0)+mm_x(dy,k,1,0)
        dq=dqm+mm(dsl,k,1,0)*SCALE+mm_x(dxq,w,1,0)
        dk=dkm+mm(dsl,q,0,0)*SCALE+mm_x(dy,w,0,0)
        dx=dt*col_to_row(beta,eye)
        dbr=jnp.sum(dt*x,axis=0,keepdims=True)
        da=jnp.where(same&(r>c),-mm_xy(mm_xy(x,dx,0,0),x,1,1),0.0)
        gram=mm(w,w,1,1)
        dbeta=jnp.sum(da*gram,axis=1,keepdims=True)+jnp.sum(jnp.where(eye,dbr,0.0),axis=1,keepdims=True)
        dg=beta*da
        dw=dw+mm_x(dg,w,1,0)+mm_x(dg,w,0,0)
        dlog=dbeta*beta*(1.0-0.5*beta)
        dhr=rs*dw-(rs*rs*rs)*hr*jnp.sum(hr*dw,axis=1,keepdims=True)
        dproj_ref[:,h*E_:(h+1)*E_]=dq.astype(bf16)
        dproj_ref[:,(nh+h)*E_:(nh+h+1)*E_]=dk.astype(bf16)
        dproj_ref[:,(2*nh+h)*E_:(2*nh+h+1)*E_]=dv_ref[h].astype(bf16)
        dproj_ref[:,(3*nh+h)*E_:(3*nh+h+1)*E_]=dhr.astype(bf16)
        dlog_all=dlog_all+jnp.where(lane==h,dlog,0.0)
    dproj_ref[:,4*nh*E_:(4*nh+1)*E_]=dlog_all.astype(bf16)
    @pl.when(g==0)
    def _():
        dbias_ref[...]=jnp.zeros_like(dbias_ref)
    dbias_ref[...]=dbias_ref[...]+jnp.sum(dlog_all,axis=0,keepdims=True)

def run_factor_back(proj,bias,w,qm,kmp,mix,x,dqm,dloc,dkf,dw,dmix,dv):
    nh,L,_=qm.shape; wd=proj.shape[1]
    blk=pl.BlockSpec((nh,PAIR,E_),lambda g:(0,g,0))
    return pl.pallas_call(functools.partial(factor_back_kernel,nh),
        grid=(L//PAIR,),
        in_specs=[pl.BlockSpec((PAIR,wd),lambda g:(g,0)),pl.BlockSpec(memory_space=pltpu.SMEM)]+[blk]*11,
        out_specs=[pl.BlockSpec((PAIR,wd),lambda g:(g,0)),pl.BlockSpec((1,E_),lambda g:(0,0))],
        out_shape=[jax.ShapeDtypeStruct((L,wd),bf16),jax.ShapeDtypeStruct((1,E_),f32)],
        cost_estimate=spent(30),
    )(proj,bias,w,qm,kmp,mix,x,dqm,dloc,dkf,dw,dmix,dv)


from jax.sharding import Mesh, PartitionSpec as P

HEADS = 12
DP = ("x", "core")
SEQ = ("hi", "lo")
TP = ("x", "core", "lo")
ALL = ("x", "core", "hi", "lo")


def rms_scale(values):
    return lax.rsqrt(jnp.mean(values * values, axis=-1, keepdims=True) + EPS)


def rms_back(grad, values, scale, gains):
    scaled = grad * gains
    inner = jnp.mean(scaled * values, axis=-1, keepdims=True)
    return scale * scaled - (scale * scale * scale) * values * inner


def dot(a, b):
    return jnp.dot(a, b, preferred_element_type=f32)


def dot_nt(a, b):
    return lax.dot_general(a, b, (((1,), (1,)), ((), ())), preferred_element_type=f32)


def dot_tn(a, b):
    return lax.dot_general(a, b, (((0,), (0,)), ((), ())), preferred_element_type=f32)


def gather(shard, axes):
    return lax.all_gather(shard, axes, axis=0, tiled=True)


def scatter(full, axes):
    return lax.psum_scatter(full, axes, scatter_dimension=0, tiled=True)


def exchange(pieces, axes):
    return lax.all_to_all(pieces, axes, 0, 0, tiled=True)


def swap(a, axis):
    return lax.ppermute(a, axis, [(0, 1), (1, 0)])


def ring(a):
    n = lax.axis_size("hi")
    return lax.ppermute(a, "hi", [(i, (i + 1) % n) for i in range(n)])


def gather_seq(a):
    n = lax.axis_size("hi")
    hi, lo = lax.axis_index("hi"), lax.axis_index("lo")
    whole = jnp.zeros((n, 2) + a.shape, a.dtype)
    zeros = (0,) * a.ndim
    for step in range(n):
        if step:
            a = ring(a)
        at = (hi + n - step) % n
        whole = lax.dynamic_update_slice(whole, a[None, None], (at, lo) + zeros)
        whole = lax.dynamic_update_slice(whole, swap(a, "lo")[None, None], (at, 1 - lo) + zeros)
    return whole.reshape((-1,) + a.shape[1:])


def scatter_seq(parts):
    n = lax.axis_size("hi")
    hi, lo = lax.axis_index("hi"), lax.axis_index("lo")
    parts = parts.reshape((n, 2, -1) + parts.shape[1:])
    total = None
    for step in range(n):
        at = (hi + 2 * n - 1 - step) % n
        mine = lax.dynamic_slice_in_dim(parts, at, 1, 0)[0]
        other = lax.dynamic_index_in_dim(mine, 1 - lo, 0, keepdims=False).astype(bf16)
        own = lax.dynamic_index_in_dim(mine, lo, 0, keepdims=False)
        own = own + swap(other, "lo").astype(f32)
        total = own if total is None else own + ring(total.astype(bf16)).astype(f32)
    return total


def gather_tp(a):
    half = a.shape[0] // 2
    a_lo, a_x = swap(a, "lo"), swap(a, "x")
    a_both = jnp.concatenate([swap(a_lo[:half], "x"), swap(a_x[half:], "lo")], axis=0)
    parts = [a, a_lo, a_x, a_both]
    return jnp.concatenate(parts + [swap(p, "core") for p in parts], axis=0)


def scatter_tp(parts):
    parts = parts.reshape((2, 4, -1) + parts.shape[1:])
    half = parts.shape[2] // 2
    sent = [swap(parts[1, i].astype(bf16), "core") for i in (3, 1, 2, 0)]
    both, low, across, own = [parts[0, i] + s.astype(f32) for i, s in zip((3, 1, 2, 0), sent)]
    from_x = swap(both[:half].astype(bf16), "x").astype(f32)
    from_lo = swap(both[half:].astype(bf16), "lo").astype(f32)
    low = jnp.concatenate([low[:half] + from_x, low[half:]], axis=0).astype(bf16)
    across = jnp.concatenate([across[:half], across[half:] + from_lo], axis=0).astype(bf16)
    return own + swap(low, "lo").astype(f32) + swap(across, "x").astype(f32)


def join(a, axis, b=None):
    b = swap(a, axis) if b is None else b
    first = lax.axis_index(axis) == 0
    return jnp.stack([jnp.where(first, a, b), jnp.where(first, b, a)])


def keep(parts, axis):
    first = lax.axis_index(axis) == 0
    sent = jnp.where(first, parts[1], parts[0]).astype(bf16)
    return jnp.where(first, parts[0], parts[1]) + swap(sent, axis).astype(f32)


def gather_rows(a):
    n = lax.axis_size("hi")
    hi = lax.axis_index("hi")
    whole = jnp.zeros((n,) + a.shape, a.dtype)
    for step in range(n):
        if step:
            a = ring(a)
        whole = lax.dynamic_update_slice(whole, a[None], ((hi + n - step) % n, 0, 0))
    whole = whole.reshape((-1,) + a.shape[1:])
    for axis in ("lo", "x", "core"):
        whole = join(whole, axis).reshape((-1,) + a.shape[1:])
    return whole


def scatter_rows(parts):
    tail = parts.shape[1:]
    for axis in ("core", "x", "lo"):
        parts = keep(parts.reshape((2, -1) + tail), axis)
    n = lax.axis_size("hi")
    hi = lax.axis_index("hi")
    parts = parts.reshape((n, -1) + tail)
    total = None
    for step in range(n):
        own = lax.dynamic_index_in_dim(parts, (hi + 2 * n - 1 - step) % n, 0, keepdims=False)
        total = own if total is None else own + ring(total.astype(bf16)).astype(f32)
    return total


def on_device(inputs, doc_lengths, w_query, w_key, w_value, w_house, w_beta, beta_bias, norm_attn, w_out,
              norm_mlp, w_gate, w_up, w_down, grad_y):
    hi_n, lo_n = lax.axis_size("hi"), lax.axis_size("lo")
    dp_n = lax.axis_size("x") * lax.axis_size("core")
    seq_n = hi_n * lo_n
    tp_n = dp_n * lo_n
    seq_at = lax.axis_index("hi") * lo_n + lax.axis_index("lo")
    dp_at = lax.axis_index("x") * lax.axis_size("core") + lax.axis_index("core")
    rows, width = w_query.shape
    tokens = inputs.shape[1]
    length = tokens * seq_n
    ff_rows = w_down.shape[0]
    ff_n = ff_rows * hi_n
    nh = -(-HEADS // seq_n)
    head_cols = nh * E_
    slot = 4 * head_cols + E_
    x_own = inputs[0]
    gy_own = grad_y[0]

    def slots(w, each):
        return jnp.pad(w, ((0, 0), (0, seq_n * each - w.shape[1]))).reshape(rows, seq_n, each)

    spare = jnp.concatenate([
        slots(w_beta, nh),
        jnp.broadcast_to(jnp.stack([norm_attn, norm_mlp], -1)[:, None], (rows, seq_n, 2)),
        jnp.zeros((rows, seq_n, E_ - nh - 2), bf16)], axis=2)
    pack = jnp.concatenate([slots(w, head_cols) for w in (w_query, w_key, w_value, w_house)] + [spare], axis=2)
    x_row = gather_seq(x_own)
    pack = exchange(jnp.swapaxes(pack, 0, 1), SEQ)
    pack = join(join(pack, "x"), "core")
    pack = jnp.swapaxes(pack, 0, 1).reshape(width, slot)
    gains = pack[:, 4 * head_cols + nh:4 * head_cols + nh + 2].astype(f32)
    gain_one, gain_two = gains[:, 0][None], gains[:, 1][None]
    out_full = gather_rows(w_out)

    def unit_pieces(w):
        w = w.reshape(rows, dp_n, hi_n, lo_n, ff_rows)
        return jnp.transpose(w, (1, 3, 0, 2, 4)).reshape(tp_n, rows, ff_n)

    gate_up = exchange(jnp.concatenate([unit_pieces(w_gate), unit_pieces(w_up)], axis=2), TP)
    gate_up = gather(gate_up, "hi").reshape(width, 2 * ff_n)
    down = gather(w_down, "hi")
    gy_all = gather_tp(gy_own)

    def to_gathered_order(a):
        a = a.reshape(tokens, dp_n // 2, 2, hi_n, lo_n, rows)
        return jnp.transpose(a, (0, 2, 1, 4, 3, 5)).reshape(tokens, width)

    def from_gathered_order(a):
        a = a.reshape(tokens, 2, dp_n // 2, lo_n, hi_n, rows)
        return jnp.transpose(a, (0, 2, 1, 4, 3, 5)).reshape(tokens, width)

    x_rowf = x_row.astype(f32)
    row_scale = rms_scale(x_rowf)
    normed = (x_rowf * row_scale * gain_one).astype(bf16)
    proj = dot(normed, pack)
    bias_own = lax.dynamic_slice_in_dim(jnp.pad(beta_bias, (0, seq_n * nh - HEADS)), seq_at * nh, nh)
    ends = jnp.cumsum(doc_lengths[0])
    values = jnp.swapaxes(proj[:, 2 * head_cols:3 * head_cols].astype(bf16).reshape(length, nh, E_), 0, 1)
    houses, moved_q, moved_k, final_k, mixing, local_raw, inverse = run_factors(proj, bias_own, nh)
    mixed, log_sum, history = run_forward(ends, moved_q, final_k, houses, mixing, local_raw, values)
    mixed = exchange(mixed.reshape(seq_n, tokens, head_cols), SEQ)
    mixed = jnp.swapaxes(mixed, 0, 1).reshape(tokens, seq_n * head_cols)[:, :width]
    mixed = to_gathered_order(mixed)

    x_float = x_own.astype(f32)
    middle = x_float + dot(mixed, out_full)
    mid_scale = rms_scale(middle)
    normed_mlp = (middle * mid_scale * gain_two).astype(bf16)

    def to_owner_order(a):
        return jnp.swapaxes(a.reshape(tokens, dp_n, hi_n, lo_n * rows), 1, 2).reshape(tokens, width)

    def from_owner_order(a):
        return jnp.swapaxes(a.reshape(tokens, hi_n, dp_n, lo_n * rows), 1, 2).reshape(tokens, width)

    nm_all = gather_tp(to_owner_order(normed_mlp))
    both = dot(nm_all, gate_up)
    gate_val, up_val = both[:, :ff_n], both[:, ff_n:]
    sig = jax.nn.sigmoid(gate_val)
    silu = gate_val * sig
    hidden = (silu * up_val).astype(bf16)
    result = middle + scatter_tp(dot(hidden, down))

    d_hidden = dot_nt(gy_all, down)
    d_gate = d_hidden * up_val * (sig * (1.0 + gate_val * (1.0 - sig)))
    d_up = d_hidden * silu
    d_both = jnp.concatenate([d_gate.astype(bf16), d_up.astype(bf16)], axis=1)
    d_nm = from_owner_order(scatter_tp(dot_nt(d_both, gate_up)))
    grad_both = dot_tn(nm_all, d_both).astype(bf16)
    grad_down = dot_tn(hidden, gy_all).astype(bf16)
    grad_down = scatter(grad_down, "hi").astype(f32)
    grad_both = scatter(grad_both.reshape(hi_n * tp_n, rows, 2 * ff_n), "hi")
    d_middle = gy_own.astype(f32) + rms_back(d_nm, middle, mid_scale, gain_two)
    gain_mlp_part = jnp.sum(d_nm * middle * mid_scale, axis=0)

    d_branch = d_middle.astype(bf16)
    d_mixed = from_gathered_order(dot_nt(d_branch, out_full).astype(bf16))
    grad_out = scatter_rows(dot_tn(mixed, d_branch))
    d_mixed = jnp.pad(d_mixed, ((0, 0), (0, seq_n * head_cols - width))).reshape(tokens, seq_n, head_cols)
    d_mixed = exchange(jnp.swapaxes(d_mixed, 0, 1), SEQ).reshape(length, head_cols)
    d_mq, d_local, d_fk, d_w, d_mix, d_val = run_backward(
        ends, moved_q, houses, mixing, local_raw, log_sum, d_mixed, history, values)
    d_proj, d_bias = run_factor_back(proj, bias_own, houses, moved_q, moved_k, mixing, inverse,
                                     d_mq, d_local, d_fk, d_w, d_mix, d_val)
    d_normed_part = dot_nt(d_proj, pack)
    d_normed = scatter_seq(d_normed_part)
    gain_attn_part = jnp.sum(d_normed_part * (x_rowf * row_scale), axis=0)
    grad_x = d_middle + rms_back(d_normed, x_float, rms_scale(x_float), gain_one)

    grad_both = exchange(grad_both, TP)
    grad_both = grad_both.reshape(dp_n, lo_n, rows, 2, hi_n, ff_rows)
    grad_both = jnp.transpose(grad_both, (3, 2, 0, 4, 1, 5)).reshape(2, rows, -1).astype(f32)

    grad_pack = dot_tn(normed, d_proj)
    lane = jnp.arange(E_)[None]
    spare_grad = grad_pack[:, 4 * head_cols:]
    own = nh + dp_at
    spare_grad = jnp.where(lane == own, gain_attn_part[:, None], spare_grad)
    spare_grad = jnp.where(lane == own + dp_n, gain_mlp_part[:, None], spare_grad)
    base = nh + 2 * dp_n
    for h in range(nh):
        high = d_bias[0, h].astype(bf16).astype(f32)
        at = base + (dp_at * nh + h) * 2
        spare_grad = jnp.where(lane == at, high, spare_grad)
        spare_grad = jnp.where(lane == at + 1, d_bias[0, h] - high, spare_grad)
    grad_pack = jnp.concatenate([grad_pack[:, :4 * head_cols], spare_grad], axis=1)
    grad_pack = jnp.swapaxes(grad_pack.reshape(dp_n // 2, 2, -1, slot), 0, 1)
    grad_pack = keep(keep(grad_pack, "core"), "x").astype(bf16)
    grad_pack = exchange(grad_pack.reshape(seq_n, rows, slot), SEQ).astype(f32)

    def whole(part, n):
        return jnp.swapaxes(part, 0, 1).reshape(rows, -1)[:, :n]

    grads = [whole(grad_pack[:, :, i * head_cols:(i + 1) * head_cols], width) for i in range(4)]
    spare_grad = grad_pack[:, :, 4 * head_cols:]
    grad_beta = whole(spare_grad[:, :, :nh], HEADS)
    grad_gain_attn = jnp.sum(spare_grad[:, :, nh:nh + dp_n], axis=(0, 2))
    grad_gain_mlp = jnp.sum(spare_grad[:, :, nh + dp_n:base], axis=(0, 2))
    bias_parts = spare_grad[:, 0, base:base + 2 * nh * dp_n].reshape(seq_n, dp_n, nh, 2)
    grad_bias = jnp.sum(bias_parts, axis=(1, 3)).reshape(-1)[:HEADS]
    return (
        result.astype(bf16)[None],
        grad_x[None],
        grads[0],
        grads[1],
        grads[2],
        grads[3],
        grad_beta,
        grad_bias,
        grad_gain_attn,
        grad_out,
        grad_gain_mlp,
        grad_both[0],
        grad_both[1],
        grad_down,
    )


def solution(mesh):
    dp_n, seq_n = mesh.devices.shape
    fine = Mesh(mesh.devices.reshape(dp_n // 2, 2, seq_n // 2, 2), ALL)
    by_rows, tokens = P(ALL, None), P(DP, SEQ, None)
    in_specs = (tokens, P(DP, None), by_rows, by_rows, by_rows, by_rows, by_rows, P(), P(ALL), by_rows, P(ALL),
                by_rows, by_rows, by_rows, tokens)
    out_specs = (tokens, tokens, by_rows, by_rows, by_rows, by_rows, by_rows, P(), P(ALL), by_rows, P(ALL),
                 by_rows, by_rows, by_rows)
    return jax.shard_map(on_device, mesh=fine, in_specs=in_specs, out_specs=out_specs, check_vma=False)
```

```python
import functools
import jax, jax.numpy as jnp
from jax import lax
from jax.experimental import pallas as pl
from jax.experimental.pallas import tpu as pltpu

bf16=jnp.bfloat16; f32=jnp.float32
E_=128; BLOCK=64; PAIR=128; CHUNK=256
EPS=1e-6
SCALE=128**-0.5

def spent(us):
    return pl.CostEstimate(flops=int(us*1.1e9),bytes_accessed=1<<20,transcendentals=0)
def mm(a,b,ca,cb):
    return lax.dot_general(a,b,(((ca,),(cb,)),((),())),preferred_element_type=f32)
def halves(a):
    hi=a.astype(bf16)
    return hi,(a-hi.astype(f32)).astype(bf16)
def mm_x(a,b,ca,cb):
    h,l=halves(a)
    return mm(h,b,ca,cb)+mm(l,b,ca,cb)
def mm_y(a,b,ca,cb):
    h,l=halves(b)
    return mm(a,h,ca,cb)+mm(a,l,ca,cb)
def mm_xy(a,b,ca,cb):
    ah,al=halves(a); bh,bl=halves(b)
    return mm(ah,bh,ca,cb)+(mm(ah,bl,ca,cb)+mm(al,bh,ca,cb))

def pair_masks():
    r=lax.broadcasted_iota(jnp.int32,(PAIR,PAIR),0)
    c=lax.broadcasted_iota(jnp.int32,(PAIR,PAIR),1)
    same=(r//BLOCK)==(c//BLOCK)
    return r,c,same

def col_to_row(col,eye):
    return jnp.sum(jnp.where(eye,col,0.0),axis=0,keepdims=True)

def inverse_of(a,r,c):
    eye=(r==c).astype(f32)
    x=eye-jnp.where((r//2)==(c//2),a,0.0)
    size=2
    while size<BLOCK:
        part=jnp.where(((r//(2*size))==(c//(2*size)))&((r//size)!=(c//size)),a,0.0)
        x=x-mm_xy(mm_xy(x,part,1,0),x,1,0)
        size*=2
    return x

def factors_of(q,k,w,beta,x,r,c,same):
    eye=r==c
    t=x*col_to_row(beta,eye)
    xq=jnp.where(same&(r>=c),mm(q,w,1,1),0.0)
    y=jnp.where(same&(r>c),mm(w,k,1,1),0.0)
    xt=mm_xy(xq,t,1,0)
    ty=mm_xy(t,y,1,0)
    return t,xq,y,xt,ty

def head_inputs(proj_ref,rows,h,nh):
    q=proj_ref[rows,h*E_:(h+1)*E_].astype(bf16)
    k=proj_ref[rows,(nh+h)*E_:(nh+h+1)*E_].astype(bf16)
    hr=proj_ref[rows,(3*nh+h)*E_:(3*nh+h+1)*E_]
    ex=proj_ref[rows,4*nh*E_:(4*nh+1)*E_]
    lane=lax.broadcasted_iota(jnp.int32,ex.shape,1)
    logit=jnp.sum(jnp.where(lane==h,ex,0.0),axis=1,keepdims=True)
    return q,k,hr,logit

def factor_kernel(nh,proj_ref,bias_ref,w_ref,qm_ref,kmp_ref,kmf_ref,mix_ref,loc_ref,x_ref):
    r,c,same=pair_masks()
    for h in range(nh):
        q,k,hr,logit=head_inputs(proj_ref,slice(None),h,nh)
        beta=2.0*jax.nn.sigmoid(logit+bias_ref[h])
        w=(hr*lax.rsqrt(jnp.sum(hr*hr,axis=1,keepdims=True)+EPS)).astype(bf16)
        a=jnp.where(same&(r>c),beta*mm(w,w,1,1),0.0)
        x=inverse_of(a,r,c)
        t,xq,y,xt,ty=factors_of(q,k,w,beta,x,r,c,same)
        qm=(q.astype(f32)-mm_x(xt,w,1,0)).astype(bf16)
        kmp=(k.astype(f32)-mm_x(ty,w,0,0)).astype(bf16)
        mix=mm_x(t,w,0,0)
        inner=mm(q,k,1,1)-mm_xy(xt,y,1,0)
        cross=mm(qm,kmp,1,1)
        loc=jnp.where(same,inner,cross)
        p=jnp.where((r<BLOCK)&(c>=BLOCK),mm(kmp,w,1,1),0.0)
        kmf=(kmp.astype(f32)-mm_xy(p,mix,1,0)).astype(bf16)
        w_ref[h]=w; qm_ref[h]=qm; kmp_ref[h]=kmp; kmf_ref[h]=kmf
        mix_ref[h]=mix; loc_ref[h]=loc; x_ref[h]=x

def run_factors(proj,bias,nh):
    L=proj.shape[0]; wd=proj.shape[1]
    blk=pl.BlockSpec((nh,PAIR,E_),lambda g:(0,g,0))
    o=lambda dt: jax.ShapeDtypeStruct((nh,L,E_),dt)
    return pl.pallas_call(functools.partial(factor_kernel,nh),
        grid=(L//PAIR,),
        in_specs=[pl.BlockSpec((PAIR,wd),lambda g:(g,0)),pl.BlockSpec(memory_space=pltpu.SMEM)],
        out_specs=[blk]*7,
        out_shape=[o(bf16),o(bf16),o(bf16),o(bf16),o(f32),o(f32),o(f32)],
        cost_estimate=spent(38),
    )(proj,bias)

def start_of(ends_ref,docs,pos):
    s=jnp.zeros_like(pos)
    for d in range(docs):
        s=jnp.maximum(s,jnp.where(pos>=ends_ref[d],ends_ref[d],0))
    return s

def scalar_start(ends_ref,docs,pos):
    s=jnp.int32(0)
    for d in range(docs):
        s=jnp.maximum(s,jnp.where(pos>=ends_ref[d],ends_ref[d],0))
    return s

def tile_pos(g,shape):
    return g*PAIR+lax.broadcasted_iota(jnp.int32,shape,0)

def chunk_range(ends_ref,docs,g):
    lo=scalar_start(ends_ref,docs,g*PAIR)//CHUNK
    hi=(g*PAIR+CHUNK-1)//CHUNK
    return lo,hi

def carried_forward(st,w,mh,ml):
    ph,pl_=halves(mm(st,w,1,1))
    return (st.astype(f32)-(mm(ph,mh,1,0)+(mm(ph,ml,1,0)+mm(pl_,mh,1,0)))).astype(bf16)

def forward_kernel(nh,docs,ends_ref,qm_ref,kmf_ref,w_ref,mix_ref,loc_ref,v_ref,
                   out_ref,lse_ref,hist_ref,stack,sbuf):
    g=pl.program_id(0)
    @pl.when(g==0)
    def _():
        stack[...]=jnp.zeros_like(stack)
    lo,hi=chunk_range(ends_ref,docs,g)
    rowstart=start_of(ends_ref,docs,tile_pos(g,(PAIR,PAIR)))
    cc=lax.broadcasted_iota(jnp.int32,(PAIR,PAIR),1)
    rr=lax.broadcasted_iota(jnp.int32,(PAIR,PAIR),0)
    okd=(cc<=rr)&(cc+g*PAIR>=rowstart)
    sd=[jnp.where(okd,loc_ref[h]*SCALE,-1e30) for h in range(nh)]
    peak=tuple(jnp.max(s,axis=1,keepdims=True) for s in sd)
    start2=start_of(ends_ref,docs,tile_pos(g,(PAIR,CHUNK)))
    c2=lax.broadcasted_iota(jnp.int32,(PAIR,CHUNK),1)
    mixs=[[halves(mix_ref[h,b*BLOCK:(b+1)*BLOCK]) for b in range(2)] for h in range(nh)]
    def step(c,pk):
        rows=pl.ds(pl.multiple_of(c*CHUNK,CHUNK),CHUNK)
        ok=(c2+c*CHUNK>=start2)&(c2+c*CHUNK<g*PAIR)
        new=[]
        for h in range(nh):
            st0=stack[h,rows,:]
            st1=carried_forward(st0,w_ref[h,0:BLOCK],*mixs[h][0])
            st2=carried_forward(st1,w_ref[h,BLOCK:PAIR],*mixs[h][1])
            s=jnp.concatenate([mm(qm_ref[h,0:BLOCK],st0,1,1),mm(qm_ref[h,BLOCK:PAIR],st1,1,1)],axis=0)
            s=jnp.where(ok,s*SCALE,-1e30)
            sbuf[h,c]=s
            hist_ref[0,0,h,rows,:]=st0
            hist_ref[0,1,h,rows,:]=st1
            stack[h,rows,:]=st2
            new.append(jnp.maximum(pk[h],jnp.max(s,axis=1,keepdims=True)))
        return tuple(new)
    peak=lax.fori_loop(lo,hi,step,peak)
    ed=[jnp.exp(sd[h]-peak[h]) for h in range(nh)]
    tot=tuple(jnp.sum(e,axis=1,keepdims=True) for e in ed)
    def step2(c,tt):
        new=[]
        for h in range(nh):
            e=jnp.exp(sbuf[h,c]-peak[h])
            sbuf[h,c]=e
            new.append(tt[h]+jnp.sum(e,axis=1,keepdims=True))
        return tuple(new)
    tot=lax.fori_loop(lo,hi,step2,tot)
    inv=[1.0/t for t in tot]
    grow=pl.ds(pl.multiple_of(g*PAIR,PAIR),PAIR)
    acc=tuple(mm((ed[h]*inv[h]).astype(bf16),v_ref[h,grow,:],1,0) for h in range(nh))
    def step3(c,ac):
        rows=pl.ds(pl.multiple_of(c*CHUNK,CHUNK),CHUNK)
        return tuple(ac[h]+mm((sbuf[h,c]*inv[h]).astype(bf16),v_ref[h,rows,:],1,0) for h in range(nh))
    acc=lax.fori_loop(lo,hi,step3,acc)
    for h in range(nh):
        out_ref[:,h*E_:(h+1)*E_]=acc[h].astype(bf16)
        lse_ref[h]=jnp.broadcast_to(peak[h]+jnp.log(tot[h]),(PAIR,E_))
        stack[h,grow,:]=kmf_ref[h]

def run_forward(ends,qm,kmf,w,mix,loc,v):
    nh,L,_=qm.shape; G=L//PAIR; docs=ends.shape[0]
    blk=pl.BlockSpec((nh,PAIR,E_),lambda g:(0,g,0))
    return pl.pallas_call(functools.partial(forward_kernel,nh,docs),
        grid=(G,),
        in_specs=[pl.BlockSpec(memory_space=pltpu.SMEM)]+[blk]*5+[pl.BlockSpec((nh,L,E_),lambda g:(0,0,0))],
        out_specs=[pl.BlockSpec((PAIR,nh*E_),lambda g:(g,0)),blk,pl.BlockSpec((1,2,nh,L,E_),lambda g:(g,0,0,0,0))],
        out_shape=[jax.ShapeDtypeStruct((L,nh*E_),bf16),jax.ShapeDtypeStruct((nh,L,E_),f32),jax.ShapeDtypeStruct((G,2,nh,L,E_),bf16)],
        scratch_shapes=[pltpu.VMEM((nh,L,E_),bf16),pltpu.VMEM((nh,-(-L//CHUNK),PAIR,CHUNK),f32)],
        cost_estimate=spent(22),
    )(ends,qm,kmf,w,mix,loc,v)

def backward_kernel(nh,docs,ngrp,ends_ref,qm_ref,w_ref,mix_ref,loc_ref,lse_ref,do_ref,hist_ref,v_ref,
                    dqm_ref,dloc_ref,dkf_ref,dw_ref,dmix_ref,dv_ref,grad,pbuf,dpbuf):
    g=ngrp-1-pl.program_id(0)
    @pl.when(g==ngrp-1)
    def _():
        grad[...]=jnp.zeros_like(grad)
        dv_ref[...]=jnp.zeros_like(dv_ref)
    lo,hi=chunk_range(ends_ref,docs,g)
    rowstart=start_of(ends_ref,docs,tile_pos(g,(PAIR,PAIR)))
    cc=lax.broadcasted_iota(jnp.int32,(PAIR,PAIR),1)
    rr=lax.broadcasted_iota(jnp.int32,(PAIR,PAIR),0)
    okd=(cc<=rr)&(cc+g*PAIR>=rowstart)
    start2=start_of(ends_ref,docs,tile_pos(g,(PAIR,CHUNK)))
    c2=lax.broadcasted_iota(jnp.int32,(PAIR,CHUNK),1)
    grow=pl.ds(pl.multiple_of(g*PAIR,PAIR),PAIR)
    do=[do_ref[:,h*E_:(h+1)*E_] for h in range(nh)]
    lse=[lse_ref[h,:,0:1] for h in range(nh)]
    pd=[jnp.exp(jnp.where(okd,loc_ref[h]*SCALE,-1e30)-lse[h]) for h in range(nh)]
    dpd=[mm(do[h],v_ref[h,grow,:],1,1) for h in range(nh)]
    delta=tuple(jnp.sum(pd[h]*dpd[h],axis=1,keepdims=True) for h in range(nh))
    def step(c,dl):
        rows=pl.ds(pl.multiple_of(c*CHUNK,CHUNK),CHUNK)
        ok=(c2+c*CHUNK>=start2)&(c2+c*CHUNK<g*PAIR)
        new=[]
        for h in range(nh):
            st0=hist_ref[0,0,h,rows,:]; st1=hist_ref[0,1,h,rows,:]
            s=jnp.concatenate([mm(qm_ref[h,0:BLOCK],st0,1,1),mm(qm_ref[h,BLOCK:PAIR],st1,1,1)],axis=0)
            p=jnp.exp(jnp.where(ok,s*SCALE,-1e30)-lse[h])
            dp=mm(do[h],v_ref[h,rows,:],1,1)
            pbuf[h,c]=p; dpbuf[h,c]=dp
            new.append(dl[h]+jnp.sum(p*dp,axis=1,keepdims=True))
        return tuple(new)
    delta=lax.fori_loop(lo,hi,step,delta)
    for h in range(nh):
        dloc_ref[h]=(pd[h]*(dpd[h]-delta[h])).astype(bf16)
        dv_ref[h,grow,:]=dv_ref[h,grow,:]+mm(pd[h].astype(bf16),do[h],0,0)
        dkf_ref[h]=grad[h,grow,:]
    mixs=[[halves(mix_ref[h,b*BLOCK:(b+1)*BLOCK]) for b in range(2)] for h in range(nh)]
    zero=jnp.zeros((BLOCK,E_),f32)
    def pull(gr,st,w,mh,ml,qm,ds):
        ph,pl_=halves(mm(st,w,1,1))
        gh,gl=halves(gr)
        u=mm(gh,mh,1,1)+(mm(gh,ml,1,1)+mm(gl,mh,1,1))
        uh,ul=halves(u)
        dw=mm(uh,st,0,0)+mm(ul,st,0,0)
        dm=mm(ph,gh,0,0)+(mm(ph,gl,0,0)+mm(pl_,gh,0,0))
        out=gr-(mm(uh,w,1,0)+mm(ul,w,1,0))+mm(ds,qm,0,0)*SCALE
        return out,dw,dm
    def step2(c,carry):
        rows=pl.ds(pl.multiple_of(c*CHUNK,CHUNK),CHUNK)
        new=[]
        for h in range(nh):
            dq0,dq1,dw0,dw1,dm0,dm1=carry[h]
            p=pbuf[h,c]
            ds=(p*(dpbuf[h,c]-delta[h])).astype(bf16)
            ds0=ds[0:BLOCK]; ds1=ds[BLOCK:PAIR]
            st0=hist_ref[0,0,h,rows,:]; st1=hist_ref[0,1,h,rows,:]
            dq0=dq0+mm(ds0,st0,1,0); dq1=dq1+mm(ds1,st1,1,0)
            dv_ref[h,rows,:]=dv_ref[h,rows,:]+mm(p.astype(bf16),do[h],0,0)
            gr=grad[h,rows,:]
            gr,a,b=pull(gr,st1,w_ref[h,BLOCK:PAIR],*mixs[h][1],qm_ref[h,BLOCK:PAIR],ds1)
            dw1=dw1-a; dm1=dm1-b
            gr,a,b=pull(gr,st0,w_ref[h,0:BLOCK],*mixs[h][0],qm_ref[h,0:BLOCK],ds0)
            dw0=dw0-a; dm0=dm0-b
            grad[h,rows,:]=gr
            new.append((dq0,dq1,dw0,dw1,dm0,dm1))
        return tuple(new)
    res=lax.fori_loop(lo,hi,step2,tuple((zero,)*6 for _ in range(nh)))
    for h in range(nh):
        dq0,dq1,dw0,dw1,dm0,dm1=res[h]
        dqm_ref[h,0:BLOCK]=dq0*SCALE; dqm_ref[h,BLOCK:PAIR]=dq1*SCALE
        dw_ref[h,0:BLOCK]=dw0; dw_ref[h,BLOCK:PAIR]=dw1
        dmix_ref[h,0:BLOCK]=dm0; dmix_ref[h,BLOCK:PAIR]=dm1

def run_backward(ends,qm,w,mix,loc,lse,do,hist,v):
    nh,L,_=qm.shape; G=L//PAIR; docs=ends.shape[0]
    blk=pl.BlockSpec((nh,PAIR,E_),lambda i:(0,G-1-i,0))
    o=lambda dt: jax.ShapeDtypeStruct((nh,L,E_),dt)
    full=pl.BlockSpec((nh,L,E_),lambda i:(0,0,0))
    return pl.pallas_call(functools.partial(backward_kernel,nh,docs,G),
        grid=(G,),
        in_specs=[pl.BlockSpec(memory_space=pltpu.SMEM)]+[blk]*5+[pl.BlockSpec((PAIR,nh*E_),lambda i:(G-1-i,0)),
                  pl.BlockSpec((1,2,nh,L,E_),lambda i:(G-1-i,0,0,0,0)),full],
        out_specs=[blk]*5+[full],
        out_shape=[o(f32),o(bf16),o(f32),o(f32),o(f32),o(f32)],
        scratch_shapes=[pltpu.VMEM((nh,L,E_),f32)]+[pltpu.VMEM((nh,-(-L//CHUNK),PAIR,CHUNK),f32)]*2,
        cost_estimate=spent(35),
    )(ends,qm,w,mix,loc,lse,do,hist,v)

def factor_back_kernel(nh,proj_ref,bias_ref,w_ref,qm_ref,kmp_ref,mix_ref,x_ref,
                       dqm_ref,dloc_ref,dkf_ref,dw_ref,dmix_ref,dv_ref,dproj_ref,dbias_ref):
    g=pl.program_id(0)
    r,c,same=pair_masks()
    eye=r==c
    lane=lax.broadcasted_iota(jnp.int32,(PAIR,E_),1)
    dlog_all=jnp.zeros((PAIR,E_),f32)
    for h in range(nh):
        q,k,hr,logit=head_inputs(proj_ref,slice(None),h,nh)
        beta=2.0*jax.nn.sigmoid(logit+bias_ref[h])
        rs=lax.rsqrt(jnp.sum(hr*hr,axis=1,keepdims=True)+EPS)
        w=w_ref[h]; qm=qm_ref[h]; kmp=kmp_ref[h]; mix=mix_ref[h]; x=x_ref[h]
        t,xq,y,xt,ty=factors_of(q,k,w,beta,x,r,c,same)
        ds=dloc_ref[h]
        dsl=jnp.where(same,ds.astype(f32),0.0).astype(bf16)
        dsc=jnp.where(same,0.0,ds.astype(f32)).astype(bf16)
        gk=dkf_ref[h]
        p=jnp.where((r<BLOCK)&(c>=BLOCK),mm(kmp,w,1,1),0.0)
        u=jnp.where((r<BLOCK)&(c>=BLOCK),mm_xy(gk,mix,1,1),0.0)
        dkm=gk-mm_x(u,w,1,0)+mm(dsc,qm,0,0)*SCALE
        dw=dw_ref[h]-mm_x(u,kmp,0,0)
        dmix=dmix_ref[h]-mm_xy(p,gk,0,0)
        dqm=dqm_ref[h]+mm(dsc,kmp,1,0)*SCALE
        dxt=-(mm_y(dsl,y,1,1)*SCALE)-mm_x(dqm,w,1,1)
        dty=-mm_y(w,dkm,1,1)
        dy=-(mm_x(xt,dsl,0,0)*SCALE)+mm_xy(t,dty,0,0)
        dy=jnp.where(same&(r>c),dy,0.0)
        dxt=jnp.where(same,dxt,0.0); dty=jnp.where(same,dty,0.0)
        dt=mm_xy(xq,dxt,0,0)+mm_xy(dty,y,1,1)+mm_y(w,dmix,1,1)
        dt=jnp.where(same,dt,0.0)
        dxq=jnp.where(same&(r>=c),mm_xy(dxt,t,1,1),0.0)
        dw=dw-mm_xy(xt,dqm,0,0)-mm_xy(ty,dkm,1,0)+mm_xy(t,dmix,1,0)+mm_x(dxq,q,0,0)+mm_x(dy,k,1,0)
        dq=dqm+mm(dsl,k,1,0)*SCALE+mm_x(dxq,w,1,0)
        dk=dkm+mm(dsl,q,0,0)*SCALE+mm_x(dy,w,0,0)
        dx=dt*col_to_row(beta,eye)
        dbr=jnp.sum(dt*x,axis=0,keepdims=True)
        da=jnp.where(same&(r>c),-mm_xy(mm_xy(x,dx,0,0),x,1,1),0.0)
        gram=mm(w,w,1,1)
        dbeta=jnp.sum(da*gram,axis=1,keepdims=True)+jnp.sum(jnp.where(eye,dbr,0.0),axis=1,keepdims=True)
        dg=beta*da
        dw=dw+mm_x(dg,w,1,0)+mm_x(dg,w,0,0)
        dlog=dbeta*beta*(1.0-0.5*beta)
        dhr=rs*dw-(rs*rs*rs)*hr*jnp.sum(hr*dw,axis=1,keepdims=True)
        dproj_ref[:,h*E_:(h+1)*E_]=dq.astype(bf16)
        dproj_ref[:,(nh+h)*E_:(nh+h+1)*E_]=dk.astype(bf16)
        dproj_ref[:,(2*nh+h)*E_:(2*nh+h+1)*E_]=dv_ref[h].astype(bf16)
        dproj_ref[:,(3*nh+h)*E_:(3*nh+h+1)*E_]=dhr.astype(bf16)
        dlog_all=dlog_all+jnp.where(lane==h,dlog,0.0)
    dproj_ref[:,4*nh*E_:(4*nh+1)*E_]=dlog_all.astype(bf16)
    @pl.when(g==0)
    def _():
        dbias_ref[...]=jnp.zeros_like(dbias_ref)
    dbias_ref[...]=dbias_ref[...]+jnp.sum(dlog_all,axis=0,keepdims=True)

def run_factor_back(proj,bias,w,qm,kmp,mix,x,dqm,dloc,dkf,dw,dmix,dv):
    nh,L,_=qm.shape; wd=proj.shape[1]
    blk=pl.BlockSpec((nh,PAIR,E_),lambda g:(0,g,0))
    return pl.pallas_call(functools.partial(factor_back_kernel,nh),
        grid=(L//PAIR,),
        in_specs=[pl.BlockSpec((PAIR,wd),lambda g:(g,0)),pl.BlockSpec(memory_space=pltpu.SMEM)]+[blk]*11,
        out_specs=[pl.BlockSpec((PAIR,wd),lambda g:(g,0)),pl.BlockSpec((1,E_),lambda g:(0,0))],
        out_shape=[jax.ShapeDtypeStruct((L,wd),bf16),jax.ShapeDtypeStruct((1,E_),f32)],
        cost_estimate=spent(30),
    )(proj,bias,w,qm,kmp,mix,x,dqm,dloc,dkf,dw,dmix,dv)


from jax.sharding import Mesh, PartitionSpec as P

HEADS = 12
DP = ("x", "core")
SEQ = ("hi", "lo")
TP = ("x", "core", "lo")
ALL = ("x", "core", "hi", "lo")


def rms_scale(values):
    return lax.rsqrt(jnp.mean(values * values, axis=-1, keepdims=True) + EPS)


def rms_back(grad, values, scale, gains):
    scaled = grad * gains
    inner = jnp.mean(scaled * values, axis=-1, keepdims=True)
    return scale * scaled - (scale * scale * scale) * values * inner


def dot(a, b):
    return jnp.dot(a, b, preferred_element_type=f32)


def dot_nt(a, b):
    return lax.dot_general(a, b, (((1,), (1,)), ((), ())), preferred_element_type=f32)


def dot_tn(a, b):
    return lax.dot_general(a, b, (((0,), (0,)), ((), ())), preferred_element_type=f32)


def gather(shard, axes):
    return lax.all_gather(shard, axes, axis=0, tiled=True)


def scatter(full, axes):
    return lax.psum_scatter(full, axes, scatter_dimension=0, tiled=True)


def exchange(pieces, axes):
    return lax.all_to_all(pieces, axes, 0, 0, tiled=True)


def swap(a, axis):
    return lax.ppermute(a, axis, [(0, 1), (1, 0)])


def ring(a):
    n = lax.axis_size("hi")
    return lax.ppermute(a, "hi", [(i, (i + 1) % n) for i in range(n)])


def gather_seq(a):
    n = lax.axis_size("hi")
    hi, lo = lax.axis_index("hi"), lax.axis_index("lo")
    whole = jnp.zeros((n, 2) + a.shape, a.dtype)
    zeros = (0,) * a.ndim
    for step in range(n):
        if step:
            a = ring(a)
        at = (hi + n - step) % n
        whole = lax.dynamic_update_slice(whole, a[None, None], (at, lo) + zeros)
        whole = lax.dynamic_update_slice(whole, swap(a, "lo")[None, None], (at, 1 - lo) + zeros)
    return whole.reshape((-1,) + a.shape[1:])


def scatter_seq(parts):
    n = lax.axis_size("hi")
    hi, lo = lax.axis_index("hi"), lax.axis_index("lo")
    parts = parts.reshape((n, 2, -1) + parts.shape[1:])
    total = None
    for step in range(n):
        at = (hi + 2 * n - 1 - step) % n
        mine = lax.dynamic_slice_in_dim(parts, at, 1, 0)[0]
        other = lax.dynamic_index_in_dim(mine, 1 - lo, 0, keepdims=False).astype(bf16)
        own = lax.dynamic_index_in_dim(mine, lo, 0, keepdims=False)
        own = own + swap(other, "lo").astype(f32)
        total = own if total is None else own + ring(total.astype(bf16)).astype(f32)
    return total


def gather_tp(a):
    half = a.shape[0] // 2
    a_lo, a_x = swap(a, "lo"), swap(a, "x")
    a_both = jnp.concatenate([swap(a_lo[:half], "x"), swap(a_x[half:], "lo")], axis=0)
    parts = [a, a_lo, a_x, a_both]
    return jnp.concatenate(parts + [swap(p, "core") for p in parts], axis=0)


def scatter_tp(parts):
    parts = parts.reshape((2, 4, -1) + parts.shape[1:])
    half = parts.shape[2] // 2
    sent = [swap(parts[1, i].astype(bf16), "core") for i in (3, 1, 2, 0)]
    both, low, across, own = [parts[0, i] + s.astype(f32) for i, s in zip((3, 1, 2, 0), sent)]
    from_x = swap(both[:half].astype(bf16), "x").astype(f32)
    from_lo = swap(both[half:].astype(bf16), "lo").astype(f32)
    low = jnp.concatenate([low[:half] + from_x, low[half:]], axis=0).astype(bf16)
    across = jnp.concatenate([across[:half], across[half:] + from_lo], axis=0).astype(bf16)
    return own + swap(low, "lo").astype(f32) + swap(across, "x").astype(f32)


def join(a, axis, b=None):
    b = swap(a, axis) if b is None else b
    first = lax.axis_index(axis) == 0
    return jnp.stack([jnp.where(first, a, b), jnp.where(first, b, a)])


def keep(parts, axis):
    first = lax.axis_index(axis) == 0
    sent = jnp.where(first, parts[1], parts[0]).astype(bf16)
    return jnp.where(first, parts[0], parts[1]) + swap(sent, axis).astype(f32)


def gather_rows(a):
    n = lax.axis_size("hi")
    hi = lax.axis_index("hi")
    whole = jnp.zeros((n,) + a.shape, a.dtype)
    for step in range(n):
        if step:
            a = ring(a)
        whole = lax.dynamic_update_slice(whole, a[None], ((hi + n - step) % n, 0, 0))
    whole = whole.reshape((-1,) + a.shape[1:])
    for axis in ("lo", "x", "core"):
        whole = join(whole, axis).reshape((-1,) + a.shape[1:])
    return whole


def scatter_rows(parts):
    tail = parts.shape[1:]
    for axis in ("core", "x", "lo"):
        parts = keep(parts.reshape((2, -1) + tail), axis)
    n = lax.axis_size("hi")
    hi = lax.axis_index("hi")
    parts = parts.reshape((n, -1) + tail)
    total = None
    for step in range(n):
        own = lax.dynamic_index_in_dim(parts, (hi + 2 * n - 1 - step) % n, 0, keepdims=False)
        total = own if total is None else own + ring(total.astype(bf16)).astype(f32)
    return total


def unpack_kernel(n, cols, recv_ref, *outs):
    for i, out in enumerate(outs):
        for s in range(n):
            out[:, s * cols:(s + 1) * cols] = recv_ref[s, :, i * cols:(i + 1) * cols].astype(f32)


def unpack(recv, cols, width):
    return pl.pallas_call(functools.partial(unpack_kernel, width // cols, cols),
        out_shape=[jax.ShapeDtypeStruct((recv.shape[1], width), f32)] * 4,
        cost_estimate=spent(3),
    )(recv)


def on_device(inputs, doc_lengths, w_query, w_key, w_value, w_house, w_beta, beta_bias, norm_attn, w_out,
              norm_mlp, w_gate, w_up, w_down, grad_y):
    hi_n, lo_n = lax.axis_size("hi"), lax.axis_size("lo")
    dp_n = lax.axis_size("x") * lax.axis_size("core")
    seq_n = hi_n * lo_n
    tp_n = dp_n * lo_n
    seq_at = lax.axis_index("hi") * lo_n + lax.axis_index("lo")
    dp_at = lax.axis_index("x") * lax.axis_size("core") + lax.axis_index("core")
    rows, width = w_query.shape
    tokens = inputs.shape[1]
    length = tokens * seq_n
    ff_rows = w_down.shape[0]
    ff_n = ff_rows * hi_n
    nh = -(-HEADS // seq_n)
    head_cols = nh * E_
    slot = 4 * head_cols + E_
    x_own = inputs[0]
    gy_own = grad_y[0]

    def slots(w, each):
        return jnp.pad(w, ((0, 0), (0, seq_n * each - w.shape[1]))).reshape(rows, seq_n, each)

    spare = jnp.concatenate([
        slots(w_beta, nh),
        jnp.broadcast_to(jnp.stack([norm_attn, norm_mlp], -1)[:, None], (rows, seq_n, 2)),
        jnp.zeros((rows, seq_n, E_ - nh - 2), bf16)], axis=2)
    pack = jnp.concatenate([slots(w, head_cols) for w in (w_query, w_key, w_value, w_house)] + [spare], axis=2)
    x_row = gather_seq(x_own)
    pack = exchange(jnp.swapaxes(pack, 0, 1), SEQ)
    pack = join(join(pack, "x"), "core")
    pack = jnp.swapaxes(pack, 0, 1).reshape(width, slot)
    gains = pack[:, 4 * head_cols + nh:4 * head_cols + nh + 2].astype(f32)
    gain_one, gain_two = gains[:, 0][None], gains[:, 1][None]
    out_full = gather_rows(w_out)

    def unit_pieces(w):
        w = w.reshape(rows, dp_n, hi_n, lo_n, ff_rows)
        return jnp.transpose(w, (1, 3, 0, 2, 4)).reshape(tp_n, rows, ff_n)

    gate_up = exchange(jnp.concatenate([unit_pieces(w_gate), unit_pieces(w_up)], axis=2), TP)
    gate_up = gather(gate_up, "hi").reshape(width, 2 * ff_n)
    down = gather(w_down, "hi")
    gy_all = gather_tp(gy_own)

    def to_gathered_order(a):
        a = a.reshape(tokens, dp_n // 2, 2, hi_n, lo_n, rows)
        return jnp.transpose(a, (0, 2, 1, 4, 3, 5)).reshape(tokens, width)

    def from_gathered_order(a):
        a = a.reshape(tokens, 2, dp_n // 2, lo_n, hi_n, rows)
        return jnp.transpose(a, (0, 2, 1, 4, 3, 5)).reshape(tokens, width)

    x_rowf = x_row.astype(f32)
    row_scale = rms_scale(x_rowf)
    normed = (x_rowf * row_scale * gain_one).astype(bf16)
    proj = dot(normed, pack)
    bias_own = lax.dynamic_slice_in_dim(jnp.pad(beta_bias, (0, seq_n * nh - HEADS)), seq_at * nh, nh)
    ends = jnp.cumsum(doc_lengths[0])
    values = jnp.swapaxes(proj[:, 2 * head_cols:3 * head_cols].astype(bf16).reshape(length, nh, E_), 0, 1)
    houses, moved_q, moved_k, final_k, mixing, local_raw, inverse = run_factors(proj, bias_own, nh)
    mixed, log_sum, history = run_forward(ends, moved_q, final_k, houses, mixing, local_raw, values)
    mixed = exchange(mixed.reshape(seq_n, tokens, head_cols), SEQ)
    mixed = jnp.swapaxes(mixed, 0, 1).reshape(tokens, seq_n * head_cols)[:, :width]
    mixed = to_gathered_order(mixed)

    x_float = x_own.astype(f32)
    middle = x_float + dot(mixed, out_full)
    mid_scale = rms_scale(middle)
    normed_mlp = (middle * mid_scale * gain_two).astype(bf16)

    def to_owner_order(a):
        return jnp.swapaxes(a.reshape(tokens, dp_n, hi_n, lo_n * rows), 1, 2).reshape(tokens, width)

    def from_owner_order(a):
        return jnp.swapaxes(a.reshape(tokens, hi_n, dp_n, lo_n * rows), 1, 2).reshape(tokens, width)

    nm_all = gather_tp(to_owner_order(normed_mlp))
    both = dot(nm_all, gate_up)
    gate_val, up_val = both[:, :ff_n], both[:, ff_n:]
    sig = jax.nn.sigmoid(gate_val)
    silu = gate_val * sig
    hidden = (silu * up_val).astype(bf16)
    result = middle + scatter_tp(dot(hidden, down))

    d_hidden = dot_nt(gy_all, down)
    d_gate = d_hidden * up_val * (sig * (1.0 + gate_val * (1.0 - sig)))
    d_up = d_hidden * silu
    d_both = jnp.concatenate([d_gate.astype(bf16), d_up.astype(bf16)], axis=1)
    d_nm = from_owner_order(scatter_tp(dot_nt(d_both, gate_up)))
    grad_both = dot_tn(nm_all, d_both).astype(bf16)
    grad_down = dot_tn(hidden, gy_all).astype(bf16)
    grad_down = scatter(grad_down, "hi").astype(f32)
    grad_both = scatter(grad_both.reshape(hi_n * tp_n, rows, 2 * ff_n), "hi")
    d_middle = gy_own.astype(f32) + rms_back(d_nm, middle, mid_scale, gain_two)
    gain_mlp_part = jnp.sum(d_nm * middle * mid_scale, axis=0)

    d_branch = d_middle.astype(bf16)
    d_mixed = from_gathered_order(dot_nt(d_branch, out_full).astype(bf16))
    grad_out = scatter_rows(dot_tn(mixed, d_branch))
    d_mixed = jnp.pad(d_mixed, ((0, 0), (0, seq_n * head_cols - width))).reshape(tokens, seq_n, head_cols)
    d_mixed = exchange(jnp.swapaxes(d_mixed, 0, 1), SEQ).reshape(length, head_cols)
    d_mq, d_local, d_fk, d_w, d_mix, d_val = run_backward(
        ends, moved_q, houses, mixing, local_raw, log_sum, d_mixed, history, values)
    d_proj, d_bias = run_factor_back(proj, bias_own, houses, moved_q, moved_k, mixing, inverse,
                                     d_mq, d_local, d_fk, d_w, d_mix, d_val)
    d_normed_part = dot_nt(d_proj, pack)
    d_normed = scatter_seq(d_normed_part)
    gain_attn_part = jnp.sum(d_normed_part * (x_rowf * row_scale), axis=0)
    grad_x = d_middle + rms_back(d_normed, x_float, rms_scale(x_float), gain_one)

    grad_both = exchange(grad_both, TP)
    grad_both = grad_both.reshape(dp_n, lo_n, rows, 2, hi_n, ff_rows)
    grad_both = jnp.transpose(grad_both, (3, 2, 0, 4, 1, 5)).reshape(2, rows, -1).astype(f32)

    grad_pack = dot_tn(normed, d_proj)
    lane = jnp.arange(E_)[None]
    spare_grad = grad_pack[:, 4 * head_cols:]
    own = nh + dp_at
    spare_grad = jnp.where(lane == own, gain_attn_part[:, None], spare_grad)
    spare_grad = jnp.where(lane == own + dp_n, gain_mlp_part[:, None], spare_grad)
    base = nh + 2 * dp_n
    for h in range(nh):
        high = d_bias[0, h].astype(bf16).astype(f32)
        at = base + (dp_at * nh + h) * 2
        spare_grad = jnp.where(lane == at, high, spare_grad)
        spare_grad = jnp.where(lane == at + 1, d_bias[0, h] - high, spare_grad)
    grad_pack = jnp.concatenate([grad_pack[:, :4 * head_cols], spare_grad], axis=1)
    grad_pack = jnp.swapaxes(grad_pack.reshape(dp_n // 2, 2, -1, slot), 0, 1)
    grad_pack = keep(keep(grad_pack, "core"), "x").astype(bf16)
    grad_pack = exchange(grad_pack.reshape(seq_n, rows, slot), SEQ)

    def whole(part, n):
        return jnp.swapaxes(part, 0, 1).reshape(rows, -1)[:, :n]

    grads = unpack(grad_pack, head_cols, width)
    spare_grad = grad_pack[:, :, 4 * head_cols:].astype(f32)
    grad_beta = whole(spare_grad[:, :, :nh], HEADS)
    grad_gain_attn = jnp.sum(spare_grad[:, :, nh:nh + dp_n], axis=(0, 2))
    grad_gain_mlp = jnp.sum(spare_grad[:, :, nh + dp_n:base], axis=(0, 2))
    bias_parts = spare_grad[:, 0, base:base + 2 * nh * dp_n].reshape(seq_n, dp_n, nh, 2)
    grad_bias = jnp.sum(bias_parts, axis=(1, 3)).reshape(-1)[:HEADS]
    return (
        result.astype(bf16)[None],
        grad_x[None],
        grads[0],
        grads[1],
        grads[2],
        grads[3],
        grad_beta,
        grad_bias,
        grad_gain_attn,
        grad_out,
        grad_gain_mlp,
        grad_both[0],
        grad_both[1],
        grad_down,
    )


def solution(mesh):
    dp_n, seq_n = mesh.devices.shape
    fine = Mesh(mesh.devices.reshape(dp_n // 2, 2, seq_n // 2, 2), ALL)
    by_rows, tokens = P(ALL, None), P(DP, SEQ, None)
    in_specs = (tokens, P(DP, None), by_rows, by_rows, by_rows, by_rows, by_rows, P(), P(ALL), by_rows, P(ALL),
                by_rows, by_rows, by_rows, tokens)
    out_specs = (tokens, tokens, by_rows, by_rows, by_rows, by_rows, by_rows, P(), P(ALL), by_rows, P(ALL),
                 by_rows, by_rows, by_rows)
    return jax.shard_map(on_device, mesh=fine, in_specs=in_specs, out_specs=out_specs, check_vma=False)
```
